32 devices in a mesh: sub: 8 (over z, y), grp: 4 (over x, core).
Axes of the slice: x: 2, y: 2, z: 4, core: 2. Of those that a mesh axis runs over, the one named last changes fastest.
Arguments:
- stiffness: bfloat16 [8, 64, 5, 256, 256], P('sub', 'grp'), may hold values from -0.0012207031 to 0.0012207031
- deflation: bfloat16 [8, 64, 16384], P('sub', None, 'grp'), may hold values from -6 to 6
- off_map: int32 [8, 3], replicated, may hold values from -2 to 2, as said below
- need_map: int32 [8, 4, 3, 4], P(None, 'grp'), may hold values from 0 to 15, as said below
- place_map: int32 [8, 4, 3, 4], P('sub', 'grp'), may hold values from 0 to 15, as said below
Outputs:
- coarse: float32 [8, 256, 256], P('sub', 'grp')
The draws below stay inside these ranges and needn't reach their ends.
Inputs may be any that keep to these rules, and one draw needn't show every extreme that they name: `off_map`: the 3 offsets of one row are distinct and nonzero. `need_map`: the 4 tile numbers of one row are distinct. `place_map`: the 4 tile numbers of one row are distinct.
All inputs are finite; a program needn't handle non-finite values.
Results may differ from the reference program's by a relative error of at most 0.0029.
Values may be sent and summed in bfloat16 or wider, within the bound.
A program may use at most 128 MiB of HBM per device.

```python
import jax
import jax.numpy as jnp
from jax import lax

TILE = 256
NVEC = 64
TD = 16
BAND = 5
NB = 3
RCH = 2
OV = 4
NBLK = 4
SUBS = 8
LAYERS = 4
ROWS_SUB = 16384


def pick_distinct(key, count, total, take):
    keys = jax.random.split(key, count)
    perms = jax.vmap(lambda one_key: jax.random.permutation(one_key, total))(keys)
    inner = 1 + jax.random.permutation(jax.random.fold_in(key, 5), total - 2)
    first = jnp.concatenate([jnp.array([0, total - 1], dtype=perms.dtype), inner.astype(perms.dtype)])
    return perms[:, :take].at[0].set(first[:take])


def draw_off_map(key, part):
    picks = pick_distinct(jax.random.fold_in(key, 17), SUBS, 2 * RCH, NB)
    return jnp.where(picks < RCH, picks - RCH, picks - RCH + 1).astype(jnp.int32)


def draw_need_map(key, part):
    picks = pick_distinct(jax.random.fold_in(key, 23), SUBS * LAYERS * NB, TD, OV)
    return picks.reshape(SUBS, LAYERS, NB, OV).astype(jnp.int32)


def draw_place_map(key, part):
    picks = pick_distinct(jax.random.fold_in(key, 29), SUBS * LAYERS * NB, TD, OV)
    return picks.reshape(SUBS, LAYERS, NB, OV).astype(jnp.int32)


def steps_of(stream_key, extent, cuts, least, top_value):
    factor_of, own = 1.0, jax.random.fold_in(stream_key, 6)
    for position, shards_of in cuts:
        steps = jnp.exp(jax.random.uniform(jax.random.fold_in(own, position), (shards_of,), jnp.float32, least / len(cuts), top_value / len(cuts)))
        factor_of = factor_of * jnp.repeat(steps, extent[position] // shards_of).reshape([-1 if axis == position else 1 for axis in range(len(extent))])
    return factor_of


def noise(own_key, dims, deviation, limit, cuts=(), kind=jnp.bfloat16):
    gain = steps_of(own_key, dims, cuts, -0.22, 0.18) if cuts else 1.0
    values = jax.random.normal(own_key, dims, jnp.float32) * deviation * gain
    return jnp.minimum(jnp.maximum(values, -limit), limit).astype(kind)


def setup_inputs(seed: int = 0) -> dict:
    streams_of = jax.random.split(jax.random.key(seed), 6)
    stiffness = noise(streams_of[0], (SUBS, LAYERS * TD, BAND, TILE, TILE), (BAND * TILE * ROWS_SUB) ** -0.5, 0.0012207031, ((0, 8), (1, 4)))
    deflation = noise(streams_of[1], (SUBS, NVEC, ROWS_SUB), 1.0, 6.0, ((0, 8), (2, 4)))
    off_map = draw_off_map(jax.random.fold_in(streams_of[5], 71), 0)
    need_map = draw_need_map(jax.random.fold_in(streams_of[5], 71), 0)
    place_map = draw_place_map(jax.random.fold_in(streams_of[5], 71), 0)
    return {"stiffness": stiffness, "deflation": deflation, "off_map": off_map, "need_map": need_map, "place_map": place_map}


def reference(stiffness, deflation, off_map, need_map, place_map):
    rim_tiles = BAND // 2
    all_tiles = LAYERS * TD
    basis_tiles = deflation.reshape(SUBS, NVEC, LAYERS, TD, TILE)
    layer_ids = jnp.arange(LAYERS, dtype=jnp.int32)[:, None]

    def subdomain_block(subdomain):
        own_basis = basis_tiles[subdomain]
        blocks = [own_basis]
        for slot_index in range(NB):
            other = jnp.mod(subdomain + off_map[subdomain, slot_index], SUBS).astype(jnp.int32)
            source = basis_tiles[other]
            needed = need_map[subdomain, :, slot_index, :]
            placed = place_map[subdomain, :, slot_index, :]
            picked = source[:, layer_ids, needed, :]
            blank_tiles = jnp.zeros_like(own_basis)
            blocks.append(blank_tiles.at[:, layer_ids, placed, :].set(picked))
        basis = jnp.concatenate(blocks, 0).reshape(NBLK * NVEC, all_tiles, TILE)
        padded = jnp.pad(basis, ((0, 0), (rim_tiles, rim_tiles), (0, 0))).astype(jnp.float32)
        local_stiffness = stiffness[subdomain]
        running = jnp.zeros((NBLK * NVEC, all_tiles, TILE), jnp.float32)
        for band_index in range(BAND):
            window = padded[:, band_index:band_index + all_tiles]
            tiles_now = local_stiffness[:, band_index].astype(jnp.float32)
            running = running + jnp.einsum("ctk,tjk->ctj", window, tiles_now)
        product_image = running.astype(jnp.bfloat16)
        flat_basis = basis.reshape(NBLK * NVEC, all_tiles * TILE)
        flat_image = product_image.reshape(NBLK * NVEC, all_tiles * TILE)
        return jnp.dot(flat_basis, flat_image.T, preferred_element_type=jnp.float32)

    return lax.map(subdomain_block, jnp.arange(SUBS, dtype=jnp.int32))
```

```python
import functools

import jax
import jax.numpy as jnp
from jax import lax
from jax.experimental import pallas as pl
from jax.experimental.pallas import tpu as pltpu
from jax.sharding import PartitionSpec as P

RCH = 2
MESH = pl.DeviceIdType.MESH
OFFSETS = [value for value in range(-RCH, RCH + 1) if value != 0]
SEND_ORDER = sorted(OFFSETS, key=lambda value: (value < 0, abs(value)))
CHUNKS = 1
NT = (((1,), (1,)), ((), ()))
NN = (((1,), (0,)), ((), ()))


def dot_nt(lhs, rhs):
    return lax.dot_general(lhs, rhs, NT, preferred_element_type=jnp.float32)


def dot_nn(lhs, rhs):
    return lax.dot_general(lhs, rhs, NN, preferred_element_type=jnp.float32)


def kernel(
    subs, layers, chunks, off_hbm, need_hbm, place_hbm, defl_ref, stiff_ref, out_ref,
    off_ref, need_ref, place_ref, a_buf, basis, image, left_image, own_tiles, outgoing, part, part_low, shares,
    in_sem, a_sem, sub_send, sub_recv, own_send, own_recv, rim_send, rim_recv, red_send, red_recv,
    *arrived,
):
    s = lax.axis_index("sub")
    g = lax.axis_index("grp")
    _, tiles, bands, rows, _ = stiff_ref.shape
    vectors = defl_ref.shape[1]
    slots = off_ref.shape[0]
    overlap = place_ref.shape[3]
    rim = bands // 2
    halo = rim * rows
    width = tiles * rows
    columns = vectors * (slots + 1)
    share = out_ref.shape[1]
    depth = vectors // chunks
    count = len(OFFSETS)
    has_left = g > 0
    has_right = g < layers - 1

    barrier = pltpu.get_barrier_semaphore()
    for offset in SEND_ORDER:
        pl.semaphore_signal(
            barrier, inc=1, device_id=(lax.rem(s + offset + subs, subs), g), device_id_type=MESH
        )
    for step in range(1, layers):
        pl.semaphore_signal(
            barrier, inc=1, device_id=(s, lax.rem(g + step, layers)), device_id_type=MESH
        )

    inputs = [
        pltpu.make_async_copy(off_hbm, off_ref, in_sem.at[0]),
        pltpu.make_async_copy(need_hbm, need_ref, in_sem.at[1]),
        pltpu.make_async_copy(place_hbm, place_ref, in_sem.at[2]),
        pltpu.make_async_copy(
            defl_ref.at[0], basis.at[0, :, pl.ds(halo, width)], in_sem.at[3]
        ),
    ]
    for copy in inputs:
        copy.start()

    def stiff_copy(t):
        return pltpu.make_async_copy(stiff_ref.at[0, t], a_buf.at[t], a_sem.at[t])

    edges = list(range(rim)) + list(range(tiles - rim, tiles))

    for buffer in arrived:
        for k in range(count):
            buffer[k * (overlap + 1) + overlap] = jnp.zeros((depth, rows), buffer.dtype)

    @pl.when(jnp.logical_not(has_left))
    def _():
        basis[:, :, 0:halo] = jnp.zeros((slots + 1, vectors, halo), basis.dtype)

    @pl.when(jnp.logical_not(has_right))
    def _():
        basis[:, :, halo + width :] = jnp.zeros((slots + 1, vectors, halo), basis.dtype)

    for copy in inputs:
        copy.wait()
    for t in range(tiles):
        stiff_copy(t).start()
    for u in range(tiles):
        own_tiles[u] = basis[0, :, halo + u * rows : halo + (u + 1) * rows]
    for k, offset in enumerate(OFFSETS):
        target = lax.rem(s + offset + subs, subs)
        for o in range(overlap):
            tile = jnp.int32(0)
            for n in range(slots):
                match = (off_ref[n, target] == -offset).astype(jnp.int32)
                tile = tile + match * need_ref[0, n, o, target]
            outgoing[k, o] = own_tiles[tile]

    pl.semaphore_wait(barrier, count + layers - 1)

    def sub_copy(k, h):
        back = count - 1 - k
        return pltpu.make_async_remote_copy(
            src_ref=outgoing.at[k, :, pl.ds(h * depth, depth)],
            dst_ref=arrived[h].at[pl.ds(back * (overlap + 1), overlap)],
            send_sem=sub_send.at[h, k],
            recv_sem=sub_recv.at[h, back],
            device_id=(lax.rem(s + OFFSETS[k] + subs, subs), g),
            device_id_type=MESH,
        )

    for h in range(chunks):
        for offset in SEND_ORDER:
            sub_copy(OFFSETS.index(offset), h).start()

    def edge_copy(blocks, lines, to_left, send, recv):
        source, target = (halo, halo + width) if to_left else (width, 0)
        return pltpu.make_async_remote_copy(
            src_ref=basis.at[blocks, lines, pl.ds(source, halo)],
            dst_ref=basis.at[blocks, lines, pl.ds(target, halo)],
            send_sem=send.at[0 if to_left else 1],
            recv_sem=recv.at[1 if to_left else 0],
            device_id=(s, g - 1 if to_left else g + 1),
            device_id_type=MESH,
        )

    def own_copy(to_left):
        return edge_copy(pl.ds(0, 1), pl.ds(0, vectors), to_left, own_send, own_recv)

    def rim_copy(h):
        return lambda to_left: edge_copy(
            pl.ds(1, slots), pl.ds(h * depth, depth), to_left, rim_send.at[h], rim_recv.at[h]
        )

    def start_pair(make):
        @pl.when(has_left)
        def _():
            make(True).start()

        @pl.when(has_right)
        def _():
            make(False).start()

    def wait_pair(make):
        @pl.when(has_left)
        def _():
            make(False).wait_recv()
            make(True).wait_send()

        @pl.when(has_right)
        def _():
            make(True).wait_recv()
            make(False).wait_send()

    start_pair(own_copy)

    def column(t):
        return t * rows if isinstance(t, int) else pl.multiple_of(t * rows, rows)

    def image_of(t):
        running = None
        for b in range(bands):
            term = dot_nt(basis[0, :, pl.ds(column(t + b), rows)], a_buf[t, b])
            running = term if running is None else running + term
        image[:, pl.ds(column(t), rows)] = running.astype(image.dtype)

    def left_of(c, blocks):
        running = None
        for b in range(bands):
            t = c - b
            if isinstance(t, int) and not 0 <= t < tiles:
                continue
            window = basis[blocks, :, pl.ds(column(t + rim), rows)]
            shape = window.shape
            term = dot_nn(window.reshape(-1, rows), a_buf[t, b])
            running = term if running is None else running + term
        left_image[blocks, :, pl.ds(column(c), rows)] = running.astype(left_image.dtype).reshape(shape)

    own_blocks, other_blocks = slice(0, 1), slice(1, slots + 1)

    def own_step(t, carry):
        stiff_copy(t).wait()
        if not isinstance(t, int) or rim <= t < tiles - rim:
            image_of(t)
        left_of(t, own_blocks)
        return carry

    inside = range(bands - 1, tiles - rim)
    for t in range(inside.start):
        own_step(t, 0)
    lax.fori_loop(inside.start, inside.stop, own_step, 0, unroll=2)
    for t in range(inside.stop, tiles):
        own_step(t, 0)
    for c in range(tiles, tiles + 2 * rim):
        left_of(c, own_blocks)
    wait_pair(own_copy)
    for t in edges:
        image_of(t)
    part[0:vectors, 0:vectors] = dot_nt(basis[0, :, halo : halo + width], image[...])

    def place(h, u, n):
        offset = off_ref[n, s]
        position = offset + RCH - (offset > 0).astype(jnp.int32)
        found = position * (overlap + 1) + overlap
        for o in range(overlap):
            hit = (place_ref[0, n, 0, o] == u).astype(jnp.int32)
            found = found + (o - overlap) * hit
        lines = slice(h * depth, (h + 1) * depth)
        basis[n + 1, lines, pl.ds(halo + column(u), rows)] = arrived[h][found]

    for h in range(chunks):
        lines = slice(h * depth, (h + 1) * depth)
        for k in range(count):
            sub_copy(k, h).wait_recv()
        for u in edges:
            for n in range(slots):
                place(h, u, n)

        def place_step(u, carry):
            for n in range(slots):
                place(h, u, n)
            return carry

        lax.fori_loop(rim, tiles - rim, place_step, 0)
        start_pair(rim_copy(h))

    for c in range(bands - 1):
        left_of(c, other_blocks)

    def rest_step(c, carry):
        left_of(c, other_blocks)
        return carry

    lax.fori_loop(bands - 1, tiles, rest_step, 0, unroll=tiles - bands + 1)
    for c in range(tiles, tiles + 2 * rim):
        left_of(c, other_blocks)
    for h in range(chunks):
        for k in range(count):
            sub_copy(k, h).wait_send()

    others = vectors * slots
    below = basis[1:, :, halo : halo + width].reshape(others, width)
    part[vectors:, 0:vectors] = dot_nt(below, image[...])

    def partial(first, last):
        lhs = left_image[:, :, first:last].reshape(columns, -1)
        return dot_nt(lhs, basis[1:, :, first:last].reshape(others, -1))

    part[:, vectors:] = partial(halo, halo + width)
    for h in range(chunks):
        wait_pair(rim_copy(h))
    part[:, vectors:] += partial(0, halo) + partial(halo + width, width + 2 * halo)
    part_low[...] = part[...].astype(part_low.dtype)

    red_copies = []
    for step in range(1, layers):
        peer = lax.rem(g + step, layers)
        red_copies.append(
            pltpu.make_async_remote_copy(
                src_ref=part_low.at[pl.ds(pl.multiple_of(peer * share, share), share)],
                dst_ref=shares.at[step - 1],
                send_sem=red_send.at[step - 1],
                recv_sem=red_recv.at[step - 1],
                device_id=(s, peer),
                device_id_type=MESH,
            )
        )
    for copy in red_copies:
        copy.start()
    for copy in red_copies:
        copy.wait()
    result = part[pl.ds(pl.multiple_of(g * share, share), share), :]
    for step in range(1, layers):
        result = result + shares[step - 1].astype(jnp.float32)
    out_ref[0] = result


def on_device(subs, layers, stiffness, deflation, off_map, need_map, place_map):
    _, tiles, bands, rows, _ = stiffness.shape
    _, vectors, width = deflation.shape
    slots, overlap = place_map.shape[2:]
    columns = vectors * (slots + 1)
    halo = (bands // 2) * rows
    share = columns // layers
    count = len(OFFSETS)
    chunks = CHUNKS
    low = deflation.dtype
    dma = pltpu.SemaphoreType.DMA
    tables = (
        off_map.T,
        need_map.transpose(1, 2, 3, 0),
        place_map.transpose(0, 2, 1, 3),
    )
    return pl.pallas_call(
        functools.partial(kernel, subs, layers, chunks),
        out_shape=pltpu.VMEM((1, share, columns), jnp.float32),
        in_specs=[pl.BlockSpec(memory_space=pl.ANY)] * 5,
        out_specs=pl.BlockSpec(memory_space=pltpu.VMEM),
        scratch_shapes=[
            *[pltpu.SMEM(table.shape, table.dtype) for table in tables],
            pltpu.VMEM((tiles, bands, rows, rows), low),
            pltpu.VMEM((slots + 1, vectors, width + 2 * halo), low),
            pltpu.VMEM((vectors, width), low),
            pltpu.VMEM((slots + 1, vectors, width + 2 * halo), low),
            pltpu.VMEM((tiles, vectors, rows), low),
            pltpu.VMEM((count, overlap, vectors, rows), low),
            pltpu.VMEM((columns, columns), jnp.float32),
            pltpu.VMEM((columns, columns), low),
            pltpu.VMEM((layers - 1, share, columns), low),
            dma((4,)),
            dma((tiles,)),
            dma((chunks, count)), dma((chunks, count)),
            dma((2,)), dma((2,)),
            dma((chunks, 2)), dma((chunks, 2)),
            dma((layers - 1,)), dma((layers - 1,)),
            *[pltpu.VMEM((count * (overlap + 1), vectors // chunks, rows), low)] * chunks,
        ],
        compiler_params=pltpu.CompilerParams(collective_id=0, has_side_effects=True),
    )(*tables, deflation, stiffness)


def solution(mesh):
    in_specs = (
        P("sub", "grp", None, None, None),
        P("sub", None, "grp"),
        P(),
        P(None, "grp", None, None),
        P("sub", "grp", None, None),
    )
    out_specs = P("sub", "grp", None)
    return jax.shard_map(
        functools.partial(on_device, mesh.shape["sub"], mesh.shape["grp"]),
        mesh=mesh,
        in_specs=in_specs,
        out_specs=out_specs,
        check_vma=False,
    )
```

```python
import functools

import jax
import jax.numpy as jnp
from jax import lax
from jax.experimental import pallas as pl
from jax.experimental.pallas import tpu as pltpu
from jax.sharding import PartitionSpec as P

RCH = 2
MESH = pl.DeviceIdType.MESH
OFFSETS = [value for value in range(-RCH, RCH + 1) if value != 0]
SEND_ORDER = sorted(OFFSETS, key=lambda value: (value < 0, abs(value)))
CHUNKS = 1
NT = (((1,), (1,)), ((), ()))
NN = (((1,), (0,)), ((), ()))


def dot_nt(lhs, rhs):
    return lax.dot_general(lhs, rhs, NT, preferred_element_type=jnp.float32)


def dot_nn(lhs, rhs):
    return lax.dot_general(lhs, rhs, NN, preferred_element_type=jnp.float32)


def kernel(
    subs, layers, chunks, off_hbm, need_hbm, place_hbm, defl_ref, stiff_ref, out_ref,
    off_ref, need_ref, place_ref, a_buf, basis, image, left_image, own_tiles, outgoing, part, part_low, shares,
    in_sem, a_sem, sub_send, sub_recv, own_send, own_recv, rim_send, rim_recv, red_send, red_recv,
    *arrived,
):
    s = lax.axis_index("sub")
    g = lax.axis_index("grp")
    _, tiles, bands, rows, _ = stiff_ref.shape
    vectors = defl_ref.shape[1]
    slots = off_ref.shape[0]
    overlap = place_ref.shape[3]
    rim = bands // 2
    halo = rim * rows
    width = tiles * rows
    columns = vectors * (slots + 1)
    share = out_ref.shape[1]
    depth = vectors // chunks
    count = len(OFFSETS)
    has_left = g > 0
    has_right = g < layers - 1

    barrier = pltpu.get_barrier_semaphore()
    for offset in SEND_ORDER:
        pl.semaphore_signal(
            barrier, inc=1, device_id=(lax.rem(s + offset + subs, subs), g), device_id_type=MESH
        )
    for step in range(1, layers):
        pl.semaphore_signal(
            barrier, inc=1, device_id=(s, lax.rem(g + step, layers)), device_id_type=MESH
        )

    inputs = [
        pltpu.make_async_copy(off_hbm, off_ref, in_sem.at[0]),
        pltpu.make_async_copy(need_hbm, need_ref, in_sem.at[1]),
        pltpu.make_async_copy(place_hbm, place_ref, in_sem.at[2]),
        pltpu.make_async_copy(
            defl_ref.at[0], basis.at[0, :, pl.ds(halo, width)], in_sem.at[3]
        ),
    ]
    for copy in inputs:
        copy.start()

    def stiff_copy(t):
        return pltpu.make_async_copy(stiff_ref.at[0, t], a_buf.at[t], a_sem.at[t])

    edges = list(range(rim)) + list(range(tiles - rim, tiles))

    for buffer in arrived:
        for k in range(count):
            buffer[k * (overlap + 1) + overlap] = jnp.zeros((depth, rows), buffer.dtype)

    @pl.when(jnp.logical_not(has_left))
    def _():
        basis[:, :, 0:halo] = jnp.zeros((slots + 1, vectors, halo), basis.dtype)

    @pl.when(jnp.logical_not(has_right))
    def _():
        basis[:, :, halo + width :] = jnp.zeros((slots + 1, vectors, halo), basis.dtype)

    for copy in inputs:
        copy.wait()
    for t in range(tiles):
        stiff_copy(t).start()
    for u in range(tiles):
        own_tiles[u] = basis[0, :, halo + u * rows : halo + (u + 1) * rows]
    for k, offset in enumerate(OFFSETS):
        target = lax.rem(s + offset + subs, subs)
        for o in range(overlap):
            tile = jnp.int32(0)
            for n in range(slots):
                match = (off_ref[n, target] == -offset).astype(jnp.int32)
                tile = tile + match * need_ref[0, n, o, target]
            outgoing[k, o] = own_tiles[tile]

    pl.semaphore_wait(barrier, count + layers - 1)

    def sub_copy(k, h):
        back = count - 1 - k
        return pltpu.make_async_remote_copy(
            src_ref=outgoing.at[k, :, pl.ds(h * depth, depth)],
            dst_ref=arrived[h].at[pl.ds(back * (overlap + 1), overlap)],
            send_sem=sub_send.at[h, k],
            recv_sem=sub_recv.at[h, back],
            device_id=(lax.rem(s + OFFSETS[k] + subs, subs), g),
            device_id_type=MESH,
        )

    for h in range(chunks):
        for offset in SEND_ORDER:
            sub_copy(OFFSETS.index(offset), h).start()

    def edge_copy(blocks, lines, to_left, send, recv):
        source, target = (halo, halo + width) if to_left else (width, 0)
        return pltpu.make_async_remote_copy(
            src_ref=basis.at[blocks, lines, pl.ds(source, halo)],
            dst_ref=basis.at[blocks, lines, pl.ds(target, halo)],
            send_sem=send.at[0 if to_left else 1],
            recv_sem=recv.at[1 if to_left else 0],
            device_id=(s, g - 1 if to_left else g + 1),
            device_id_type=MESH,
        )

    def own_copy(to_left):
        return edge_copy(pl.ds(0, 1), pl.ds(0, vectors), to_left, own_send, own_recv)

    def rim_copy(h):
        return lambda to_left: edge_copy(
            pl.ds(1, slots), pl.ds(h * depth, depth), to_left, rim_send.at[h], rim_recv.at[h]
        )

    def start_pair(make):
        @pl.when(has_left)
        def _():
            make(True).start()

        @pl.when(has_right)
        def _():
            make(False).start()

    def wait_pair(make):
        @pl.when(has_left)
        def _():
            make(False).wait_recv()
            make(True).wait_send()

        @pl.when(has_right)
        def _():
            make(True).wait_recv()
            make(False).wait_send()

    start_pair(own_copy)

    def column(t):
        return t * rows if isinstance(t, int) else pl.multiple_of(t * rows, rows)

    def image_of(t):
        running = None
        for b in range(bands):
            term = dot_nt(basis[0, :, pl.ds(column(t + b), rows)], a_buf[t, b])
            running = term if running is None else running + term
        image[t] = running.astype(image.dtype)

    def left_of(c, blocks, lines):
        running = None
        for b in range(bands):
            t = c - b
            if isinstance(t, int) and not 0 <= t < tiles:
                continue
            window = basis[blocks, :, pl.ds(column(t + rim), rows)]
            term = dot_nn(window.reshape(-1, rows), a_buf[t, b])
            running = term if running is None else running + term
        left_image[c, lines] = running.astype(left_image.dtype)

    own = slice(0, 1), slice(0, vectors)
    others = slice(1, slots + 1), slice(vectors, columns)

    def own_step(t, carry):
        stiff_copy(t).wait()
        if not isinstance(t, int) or rim <= t < tiles - rim:
            image_of(t)
        left_of(t, *own)
        return carry

    inside = range(bands - 1, tiles - rim)
    for t in range(inside.start):
        own_step(t, 0)
    lax.fori_loop(inside.start, inside.stop, own_step, 0, unroll=len(inside))
    for t in range(inside.stop, tiles):
        own_step(t, 0)
    for c in range(tiles, tiles + 2 * rim):
        left_of(c, *own)
    wait_pair(own_copy)
    for t in edges:
        image_of(t)
    corner = None
    for t in range(tiles):
        term = dot_nt(basis[0, :, halo + t * rows : halo + (t + 1) * rows], image[t])
        corner = term if corner is None else corner + term
    part[0:vectors, 0:vectors] = corner

    def first_of(n):
        offset = off_ref[n, s]
        return (offset + RCH - (offset > 0).astype(jnp.int32)) * (overlap + 1)

    def place(h, u, n):
        found = first_of(n) + overlap
        for o in range(overlap):
            hit = (place_ref[0, n, 0, o] == u).astype(jnp.int32)
            found = found + (o - overlap) * hit
        lines = slice(h * depth, (h + 1) * depth)
        basis[n + 1, lines, pl.ds(halo + column(u), rows)] = arrived[h][found]

    for h in range(chunks):
        lines = slice(h * depth, (h + 1) * depth)
        for k in range(count):
            sub_copy(k, h).wait_recv()
        for u in edges:
            for n in range(slots):
                place(h, u, n)

        def place_step(u, carry):
            for n in range(slots):
                place(h, u, n)
            return carry

        lax.fori_loop(rim, tiles - rim, place_step, 0)
        start_pair(rim_copy(h))

    for c in range(bands - 1):
        left_of(c, *others)

    def rest_step(c, carry):
        left_of(c, *others)
        return carry

    lax.fori_loop(bands - 1, tiles, rest_step, 0, unroll=tiles - bands + 1)
    for c in range(tiles, tiles + 2 * rim):
        left_of(c, *others)
    for h in range(chunks):
        for k in range(count):
            sub_copy(k, h).wait_send()

    for n in range(slots):
        low = below = None
        for o in range(overlap):
            tile = jnp.concatenate([buffer[first_of(n) + o] for buffer in arrived])
            spot = place_ref[0, n, 0, o]
            term = dot_nt(tile, image[spot])
            low = term if low is None else low + term
            term = dot_nt(left_image[rim + spot], tile)
            below = term if below is None else below + term
        lines = slice((n + 1) * vectors, (n + 2) * vectors)
        part[lines, 0:vectors] = low
        part[:, lines] = below

    def edge_partial(tile):
        right = basis[1:, :, tile * rows : (tile + 1) * rows].reshape(-1, rows)
        return dot_nt(left_image[tile], right)

    for h in range(chunks):
        wait_pair(rim_copy(h))
    sides = None
    for tile in list(range(rim)) + list(range(tiles + rim, tiles + 2 * rim)):
        term = edge_partial(tile)
        sides = term if sides is None else sides + term
    part[:, vectors:] += sides
    part_low[...] = part[...].astype(part_low.dtype)

    red_copies = []
    for step in range(1, layers):
        peer = lax.rem(g + step, layers)
        red_copies.append(
            pltpu.make_async_remote_copy(
                src_ref=part_low.at[pl.ds(pl.multiple_of(peer * share, share), share)],
                dst_ref=shares.at[step - 1],
                send_sem=red_send.at[step - 1],
                recv_sem=red_recv.at[step - 1],
                device_id=(s, peer),
                device_id_type=MESH,
            )
        )
    for copy in red_copies:
        copy.start()
    for copy in red_copies:
        copy.wait()
    result = part[pl.ds(pl.multiple_of(g * share, share), share), :]
    for step in range(1, layers):
        result = result + shares[step - 1].astype(jnp.float32)
    out_ref[0] = result


def on_device(subs, layers, stiffness, deflation, off_map, need_map, place_map):
    _, tiles, bands, rows, _ = stiffness.shape
    _, vectors, width = deflation.shape
    slots, overlap = place_map.shape[2:]
    columns = vectors * (slots + 1)
    halo = (bands // 2) * rows
    share = columns // layers
    count = len(OFFSETS)
    chunks = CHUNKS
    low = deflation.dtype
    dma = pltpu.SemaphoreType.DMA
    tables = (
        off_map.T,
        need_map.transpose(1, 2, 3, 0),
        place_map.transpose(0, 2, 1, 3),
    )
    return pl.pallas_call(
        functools.partial(kernel, subs, layers, chunks),
        out_shape=pltpu.VMEM((1, share, columns), jnp.float32),
        in_specs=[pl.BlockSpec(memory_space=pl.ANY)] * 5,
        out_specs=pl.BlockSpec(memory_space=pltpu.VMEM),
        scratch_shapes=[
            *[pltpu.SMEM(table.shape, table.dtype) for table in tables],
            pltpu.VMEM((tiles, bands, rows, rows), low),
            pltpu.VMEM((slots + 1, vectors, width + 2 * halo), low),
            pltpu.VMEM((tiles, vectors, rows), low),
            pltpu.VMEM((tiles + 2 * (bands // 2), columns, rows), low),
            pltpu.VMEM((tiles, vectors, rows), low),
            pltpu.VMEM((count, overlap, vectors, rows), low),
            pltpu.VMEM((columns, columns), jnp.float32),
            pltpu.VMEM((columns, columns), low),
            pltpu.VMEM((layers - 1, share, columns), low),
            dma((4,)),
            dma((tiles,)),
            dma((chunks, count)), dma((chunks, count)),
            dma((2,)), dma((2,)),
            dma((chunks, 2)), dma((chunks, 2)),
            dma((layers - 1,)), dma((layers - 1,)),
            *[pltpu.VMEM((count * (overlap + 1), vectors // chunks, rows), low)] * chunks,
        ],
        compiler_params=pltpu.CompilerParams(collective_id=0, has_side_effects=True),
    )(*tables, deflation, stiffness)


def solution(mesh):
    in_specs = (
        P("sub", "grp", None, None, None),
        P("sub", None, "grp"),
        P(),
        P(None, "grp", None, None),
        P("sub", "grp", None, None),
    )
    out_specs = P("sub", "grp", None)
    return jax.shard_map(
        functools.partial(on_device, mesh.shape["sub"], mesh.shape["grp"]),
        mesh=mesh,
        in_specs=in_specs,
        out_specs=out_specs,
        check_vma=False,
    )
```

```python
import functools

import jax
import jax.numpy as jnp
from jax import lax
from jax.experimental import pallas as pl
from jax.experimental.pallas import tpu as pltpu
from jax.sharding import PartitionSpec as P

RCH = 2
MESH = pl.DeviceIdType.MESH
OFFSETS = [value for value in range(-RCH, RCH + 1) if value != 0]
SEND_ORDER = sorted(OFFSETS, key=lambda value: (value < 0, abs(value)))
NEAR_FIRST = [1, 2, -2, -1]
NT = (((1,), (1,)), ((), ()))
NN = (((1,), (0,)), ((), ()))


def dot_nt(lhs, rhs):
    return lax.dot_general(lhs, rhs, NT, preferred_element_type=jnp.float32)


def dot_nn(lhs, rhs):
    return lax.dot_general(lhs, rhs, NN, preferred_element_type=jnp.float32)


def kernel(
    subs, layers, off_hbm, need_hbm, place_hbm, defl_ref, stiff_ref, out_ref,
    off_ref, need_ref, place_ref, a_buf, basis, image, left_image, own_tiles, outgoing, arrived,
    rim_out, rim_in, found_at, rim_found_at, part, part_low, shares,
    in_sem, a_sem, sub_send, sub_recv, own_send, own_recv, rim_send, rim_recv, red_send, red_recv,
):
    s = lax.axis_index("sub")
    g = lax.axis_index("grp")
    _, tiles, bands, rows, _ = stiff_ref.shape
    vectors = defl_ref.shape[1]
    slots = off_ref.shape[0]
    overlap = place_ref.shape[3]
    rim = bands // 2
    halo = rim * rows
    width = tiles * rows
    columns = vectors * (slots + 1)
    share = out_ref.shape[1]
    count = len(OFFSETS)
    has_left = g > 0
    has_right = g < layers - 1

    barrier = pltpu.get_barrier_semaphore()
    for offset in SEND_ORDER:
        pl.semaphore_signal(
            barrier, inc=1, device_id=(lax.rem(s + offset + subs, subs), g), device_id_type=MESH
        )
    for step in range(1, layers):
        pl.semaphore_signal(
            barrier, inc=1, device_id=(s, lax.rem(g + step, layers)), device_id_type=MESH
        )

    inputs = [
        pltpu.make_async_copy(off_hbm, off_ref, in_sem.at[0]),
        pltpu.make_async_copy(need_hbm, need_ref, in_sem.at[1]),
        pltpu.make_async_copy(place_hbm, place_ref, in_sem.at[2]),
        pltpu.make_async_copy(
            defl_ref.at[0], basis.at[0, :, pl.ds(halo, width)], in_sem.at[3]
        ),
    ]
    for copy in inputs:
        copy.start()

    def stiff_copy(t):
        return pltpu.make_async_copy(stiff_ref.at[0, t], a_buf.at[t], a_sem.at[t])

    edges = list(range(rim)) + list(range(tiles - rim, tiles))

    for k in range(count):
        arrived[k * (overlap + 1) + overlap] = jnp.zeros((vectors, rows), arrived.dtype)

    @pl.when(jnp.logical_not(has_left))
    def _():
        basis[0, :, 0:halo] = jnp.zeros((vectors, halo), basis.dtype)
        rim_in[:, :, 0:halo] = jnp.zeros((count, vectors, halo), rim_in.dtype)

    @pl.when(jnp.logical_not(has_right))
    def _():
        basis[0, :, halo + width :] = jnp.zeros((vectors, halo), basis.dtype)
        rim_in[:, :, halo:] = jnp.zeros((count, vectors, halo), rim_in.dtype)

    for copy in inputs:
        copy.wait()
    for t in range(tiles):
        stiff_copy(t).start()
    for u in range(tiles):
        own_tiles[u] = basis[0, :, halo + u * rows : halo + (u + 1) * rows]
    for k, offset in enumerate(OFFSETS):
        target = lax.rem(s + offset + subs, subs)
        for o in range(overlap):
            tile = jnp.int32(0)
            for n in range(slots):
                match = (off_ref[n, target] == -offset).astype(jnp.int32)
                tile = tile + match * need_ref[0, n, o, target]
            outgoing[k, o] = own_tiles[tile]

    pl.semaphore_wait(barrier, count + layers - 1)

    def sub_copy(k, offset):
        back = count - 1 - k
        return pltpu.make_async_remote_copy(
            src_ref=outgoing.at[k],
            dst_ref=arrived.at[pl.ds(back * (overlap + 1), overlap)],
            send_sem=sub_send.at[k],
            recv_sem=sub_recv.at[back],
            device_id=(lax.rem(s + offset + subs, subs), g),
            device_id_type=MESH,
        )

    lower = s < subs // 2
    for near, far in zip(NEAR_FIRST, SEND_ORDER):
        k, offset = OFFSETS.index(near), near
        if near != far:
            k = jnp.where(lower, k, OFFSETS.index(far))
            offset = jnp.where(lower, near, far)
        sub_copy(k, offset).start()

    def own_copy(to_left):
        source, target = (halo, halo + width) if to_left else (width, 0)
        return pltpu.make_async_remote_copy(
            src_ref=basis.at[0, :, pl.ds(source, halo)],
            dst_ref=basis.at[0, :, pl.ds(target, halo)],
            send_sem=own_send.at[0 if to_left else 1],
            recv_sem=own_recv.at[1 if to_left else 0],
            device_id=(s, g - 1 if to_left else g + 1),
            device_id_type=MESH,
        )

    def rim_copy(k):
        def make(to_left):
            source, target = (0, halo) if to_left else (halo, 0)
            return pltpu.make_async_remote_copy(
                src_ref=rim_out.at[k, :, pl.ds(source, halo)],
                dst_ref=rim_in.at[k, :, pl.ds(target, halo)],
                send_sem=rim_send.at[k, 0 if to_left else 1],
                recv_sem=rim_recv.at[k, 1 if to_left else 0],
                device_id=(s, g - 1 if to_left else g + 1),
                device_id_type=MESH,
            )

        return make

    def start_pair(make):
        @pl.when(has_left)
        def _():
            make(True).start()

        @pl.when(has_right)
        def _():
            make(False).start()

    def wait_pair(make):
        @pl.when(has_left)
        def _():
            make(False).wait_recv()
            make(True).wait_send()

        @pl.when(has_right)
        def _():
            make(True).wait_recv()
            make(False).wait_send()

    start_pair(own_copy)

    def column(t):
        return t * rows if isinstance(t, int) else pl.multiple_of(t * rows, rows)

    def first_of(n):
        offset = off_ref[n, s]
        return (offset + RCH - (offset > 0).astype(jnp.int32)) * (overlap + 1)

    def image_of(t):
        running = None
        for b in range(bands):
            term = dot_nt(basis[0, :, pl.ds(column(t + b), rows)], a_buf[t, b])
            running = term if running is None else running + term
        image[t] = running.astype(image.dtype)

    def left_of(c, blocks, lines):
        running = None
        for b in range(bands):
            t = c - b
            if isinstance(t, int) and not 0 <= t < tiles:
                continue
            window = basis[blocks, :, pl.ds(column(t + rim), rows)]
            term = dot_nn(window.reshape(-1, rows), a_buf[t, b])
            running = term if running is None else running + term
        left_image[c, lines] = running.astype(left_image.dtype)

    own = slice(0, 1), slice(0, vectors)
    others = slice(1, slots + 1), slice(vectors, columns)

    blank = overlap
    hits = [
        [[(place_ref[0, n, 0, o] == u).astype(jnp.int32) for o in range(overlap)] for n in range(slots)]
        for u in range(tiles)
    ]
    shift = [
        [sum((o - blank) * hits[u][n][o] for o in range(overlap)) for n in range(slots)]
        for u in range(tiles)
    ]
    for n in range(slots):
        for u in range(tiles):
            found_at[n * tiles + u] = first_of(n) + blank + shift[u][n]
    for k, offset in enumerate(OFFSETS):
        for i, u in enumerate(edges):
            spot = k * (overlap + 1) + blank
            for n in range(slots):
                spot = spot + (off_ref[n, s] == offset).astype(jnp.int32) * shift[u][n]
            rim_found_at[k * len(edges) + i] = spot

    group = bands - 1
    for first in range(0, tiles, group):
        for t in range(first, min(first + group, tiles)):
            stiff_copy(t).wait()
        for t in range(first, min(first + group, tiles)):
            if rim <= t < tiles - rim:
                image_of(t)
            left_of(t, *own)
    for c in range(tiles, tiles + 2 * rim):
        left_of(c, *own)
    wait_pair(own_copy)
    for t in edges:
        image_of(t)
    corner = None
    for t in range(tiles):
        term = dot_nt(basis[0, :, halo + t * rows : halo + (t + 1) * rows], image[t])
        corner = term if corner is None else corner + term
    part[0:vectors, 0:vectors] = corner

    for k in reversed(range(count)):
        sub_copy(count - 1 - k, OFFSETS[count - 1 - k]).wait_recv()
        for i in range(len(edges)):
            tile = jnp.zeros((vectors, rows), arrived.dtype)
            for o in range(overlap):
                spot = k * (overlap + 1) + o
                tile = jnp.where(rim_found_at[k * len(edges) + i] == spot, arrived[spot], tile)
            rim_out[k, :, i * rows : (i + 1) * rows] = tile
        if k < count - 1:
            start_pair(rim_copy(k + 1))
    for u in range(tiles):
        for n in range(slots):
            spot = halo + u * rows
            basis[n + 1, :, spot : spot + rows] = arrived[found_at[n * tiles + u]]
    start_pair(rim_copy(0))
    for c in range(tiles + 2 * rim):
        left_of(c, *others)
    for k in range(count):
        sub_copy(k, OFFSETS[k]).wait_send()

    for n in range(slots):
        low = below = None
        for o in range(overlap):
            tile = arrived[first_of(n) + o]
            spot = place_ref[0, n, 0, o]
            term = dot_nt(tile, image[spot])
            low = term if low is None else low + term
            term = dot_nt(left_image[rim + spot], tile)
            below = term if below is None else below + term
        lines = slice((n + 1) * vectors, (n + 2) * vectors)
        part[lines, 0:vectors] = low
        part[:, lines] = below

    def edge_partial(i):
        right = jnp.concatenate(
            [
                rim_in[off_ref[n, s] + RCH - (off_ref[n, s] > 0).astype(jnp.int32), :, i * rows : (i + 1) * rows]
                for n in range(slots)
            ]
        )
        return dot_nt(left_image[i if i < rim else tiles + i], right)

    for k in range(count):
        wait_pair(rim_copy(k))
    sides = None
    for i in range(2 * rim):
        term = edge_partial(i)
        sides = term if sides is None else sides + term
    part[:, vectors:] += sides
    part_low[...] = part[...].astype(part_low.dtype)

    red_copies = []
    for step in range(1, layers):
        peer = lax.rem(g + step, layers)
        red_copies.append(
            pltpu.make_async_remote_copy(
                src_ref=part_low.at[pl.ds(pl.multiple_of(peer * share, share), share)],
                dst_ref=shares.at[step - 1],
                send_sem=red_send.at[step - 1],
                recv_sem=red_recv.at[step - 1],
                device_id=(s, peer),
                device_id_type=MESH,
            )
        )
    for copy in red_copies:
        copy.start()
    for copy in red_copies:
        copy.wait()
    result = part[pl.ds(pl.multiple_of(g * share, share), share), :]
    for step in range(1, layers):
        result = result + shares[step - 1].astype(jnp.float32)
    out_ref[0] = result


def on_device(subs, layers, stiffness, deflation, off_map, need_map, place_map):
    _, tiles, bands, rows, _ = stiffness.shape
    _, vectors, width = deflation.shape
    slots, overlap = place_map.shape[2:]
    columns = vectors * (slots + 1)
    halo = (bands // 2) * rows
    share = columns // layers
    count = len(OFFSETS)
    low = deflation.dtype
    dma = pltpu.SemaphoreType.DMA
    tables = (
        off_map.T,
        need_map.transpose(1, 2, 3, 0),
        place_map.transpose(0, 2, 1, 3),
    )
    return pl.pallas_call(
        functools.partial(kernel, subs, layers),
        out_shape=pltpu.VMEM((1, share, columns), jnp.float32),
        in_specs=[pl.BlockSpec(memory_space=pl.ANY)] * 5,
        out_specs=pl.BlockSpec(memory_space=pltpu.VMEM),
        scratch_shapes=[
            *[pltpu.SMEM(table.shape, table.dtype) for table in tables],
            pltpu.VMEM((tiles, bands, rows, rows), low),
            pltpu.VMEM((slots + 1, vectors, width + 2 * halo), low),
            pltpu.VMEM((tiles, vectors, rows), low),
            pltpu.VMEM((tiles + 2 * (bands // 2), columns, rows), low),
            pltpu.VMEM((tiles, vectors, rows), low),
            pltpu.VMEM((count, overlap, vectors, rows), low),
            pltpu.VMEM((count * (overlap + 1), vectors, rows), low),
            pltpu.VMEM((count, vectors, 2 * halo), low),
            pltpu.VMEM((count, vectors, 2 * halo), low),
            pltpu.SMEM((slots * tiles,), jnp.int32),
            pltpu.SMEM((count * 2 * (bands // 2),), jnp.int32),
            pltpu.VMEM((columns, columns), jnp.float32),
            pltpu.VMEM((columns, columns), low),
            pltpu.VMEM((layers - 1, share, columns), low),
            dma((4,)),
            dma((tiles,)),
            dma((count,)), dma((count,)),
            dma((2,)), dma((2,)),
            dma((count, 2)), dma((count, 2)),
            dma((layers - 1,)), dma((layers - 1,)),
        ],
        compiler_params=pltpu.CompilerParams(collective_id=0, has_side_effects=True),
    )(*tables, deflation, stiffness)


def solution(mesh):
    in_specs = (
        P("sub", "grp", None, None, None),
        P("sub", None, "grp"),
        P(),
        P(None, "grp", None, None),
        P("sub", "grp", None, None),
    )
    out_specs = P("sub", "grp", None)
    return jax.shard_map(
        functools.partial(on_device, mesh.shape["sub"], mesh.shape["grp"]),
        mesh=mesh,
        in_specs=in_specs,
        out_specs=out_specs,
        check_vma=False,
    )
```

```python
import functools

import jax
import jax.numpy as jnp
from jax import lax
from jax.experimental import pallas as pl
from jax.experimental.pallas import tpu as pltpu
from jax.sharding import PartitionSpec as P

RCH = 2
MESH = pl.DeviceIdType.MESH
OFFSETS = [value for value in range(-RCH, RCH + 1) if value != 0]
SEND_ORDER = sorted(OFFSETS, key=lambda value: (value < 0, abs(value)))
NEAR_FIRST = [1, 2, -2, -1]
ARRIVALS = [OFFSETS.index(-value) for value in SEND_ORDER]
NT = (((1,), (1,)), ((), ()))
NN = (((1,), (0,)), ((), ()))


def dot_nt(lhs, rhs):
    return lax.dot_general(lhs, rhs, NT, preferred_element_type=jnp.float32)


def dot_nn(lhs, rhs):
    return lax.dot_general(lhs, rhs, NN, preferred_element_type=jnp.float32)


def kernel(
    subs, layers, off_hbm, need_hbm, place_hbm, defl_ref, stiff_ref, out_ref,
    off_ref, need_ref, place_ref, a_buf, basis, image, left_image, own_tiles, outgoing, arrived,
    rim_out, rim_in, found_at, rim_found_at, part, part_low, shares,
    in_sem, a_sem, sub_send, sub_recv, own_send, own_recv, rim_send, rim_recv, red_send, red_recv,
):
    s = lax.axis_index("sub")
    g = lax.axis_index("grp")
    _, tiles, bands, rows, _ = stiff_ref.shape
    vectors = defl_ref.shape[1]
    slots = off_ref.shape[0]
    overlap = place_ref.shape[3]
    rim = bands // 2
    halo = rim * rows
    width = tiles * rows
    columns = vectors * (slots + 1)
    share = out_ref.shape[1]
    count = len(OFFSETS)
    has_left = g > 0
    has_right = g < layers - 1

    barrier = pltpu.get_barrier_semaphore()
    for offset in SEND_ORDER:
        pl.semaphore_signal(
            barrier, inc=1, device_id=(lax.rem(s + offset + subs, subs), g), device_id_type=MESH
        )
    for step in range(1, layers):
        pl.semaphore_signal(
            barrier, inc=1, device_id=(s, lax.rem(g + step, layers)), device_id_type=MESH
        )

    inputs = [
        pltpu.make_async_copy(off_hbm, off_ref, in_sem.at[0]),
        pltpu.make_async_copy(need_hbm, need_ref, in_sem.at[1]),
        pltpu.make_async_copy(place_hbm, place_ref, in_sem.at[2]),
        pltpu.make_async_copy(
            defl_ref.at[0], basis.at[0, :, pl.ds(halo, width)], in_sem.at[3]
        ),
    ]
    for copy in inputs:
        copy.start()

    def stiff_copy(t):
        return pltpu.make_async_copy(stiff_ref.at[0, t], a_buf.at[t], a_sem.at[t])

    edges = list(range(rim)) + list(range(tiles - rim, tiles))

    for k in range(count):
        arrived[k * (overlap + 1) + overlap] = jnp.zeros((vectors, rows), arrived.dtype)

    @pl.when(jnp.logical_not(has_left))
    def _():
        basis[0, :, 0:halo] = jnp.zeros((vectors, halo), basis.dtype)
        rim_in[:, 0] = jnp.zeros((count, vectors, halo), rim_in.dtype)

    @pl.when(jnp.logical_not(has_right))
    def _():
        basis[0, :, halo + width :] = jnp.zeros((vectors, halo), basis.dtype)
        rim_in[:, 1] = jnp.zeros((count, vectors, halo), rim_in.dtype)

    for copy in inputs:
        copy.wait()
    for t in range(tiles):
        stiff_copy(t).start()
    for u in range(tiles):
        own_tiles[u] = basis[0, :, halo + u * rows : halo + (u + 1) * rows]
    for k, offset in enumerate(OFFSETS):
        target = lax.rem(s + offset + subs, subs)
        for o in range(overlap):
            tile = jnp.int32(0)
            for n in range(slots):
                match = (off_ref[n, target] == -offset).astype(jnp.int32)
                tile = tile + match * need_ref[0, n, o, target]
            outgoing[k, o] = own_tiles[tile]

    pl.semaphore_wait(barrier, count + layers - 1)

    def sub_copy(k, offset):
        back = count - 1 - k
        return pltpu.make_async_remote_copy(
            src_ref=outgoing.at[k],
            dst_ref=arrived.at[pl.ds(back * (overlap + 1), overlap)],
            send_sem=sub_send.at[k],
            recv_sem=sub_recv.at[back],
            device_id=(lax.rem(s + offset + subs, subs), g),
            device_id_type=MESH,
        )

    lower = s < subs // 2
    for near, far in zip(NEAR_FIRST, SEND_ORDER):
        k, offset = OFFSETS.index(near), near
        if near != far:
            k = jnp.where(lower, k, OFFSETS.index(far))
            offset = jnp.where(lower, near, far)
        sub_copy(k, offset).start()

    def own_copy(to_left):
        source, target = (halo, halo + width) if to_left else (width, 0)
        return pltpu.make_async_remote_copy(
            src_ref=basis.at[0, :, pl.ds(source, halo)],
            dst_ref=basis.at[0, :, pl.ds(target, halo)],
            send_sem=own_send.at[0 if to_left else 1],
            recv_sem=own_recv.at[1 if to_left else 0],
            device_id=(s, g - 1 if to_left else g + 1),
            device_id_type=MESH,
        )

    def rim_copy(k):
        def make(to_left):
            source, target = (0, 1) if to_left else (1, 0)
            return pltpu.make_async_remote_copy(
                src_ref=rim_out.at[k, source],
                dst_ref=rim_in.at[k, target],
                send_sem=rim_send.at[k, 0 if to_left else 1],
                recv_sem=rim_recv.at[k, 1 if to_left else 0],
                device_id=(s, g - 1 if to_left else g + 1),
                device_id_type=MESH,
            )

        return make

    def start_pair(make):
        @pl.when(has_left)
        def _():
            make(True).start()

        @pl.when(has_right)
        def _():
            make(False).start()

    def wait_pair(make):
        @pl.when(has_left)
        def _():
            make(False).wait_recv()
            make(True).wait_send()

        @pl.when(has_right)
        def _():
            make(True).wait_recv()
            make(False).wait_send()

    start_pair(own_copy)

    def column(t):
        return t * rows if isinstance(t, int) else pl.multiple_of(t * rows, rows)

    def first_of(n):
        offset = off_ref[n, s]
        return (offset + RCH - (offset > 0).astype(jnp.int32)) * (overlap + 1)

    def image_of(t):
        running = None
        for b in range(bands):
            term = dot_nt(basis[0, :, pl.ds(column(t + b), rows)], a_buf[t, b])
            running = term if running is None else running + term
        image[t] = running.astype(image.dtype)

    def left_of(c, blocks, lines):
        running = None
        for b in range(bands):
            t = c - b
            if isinstance(t, int) and not 0 <= t < tiles:
                continue
            window = basis[blocks, :, pl.ds(column(t + rim), rows)]
            term = dot_nn(window.reshape(-1, rows), a_buf[t, b])
            running = term if running is None else running + term
        left_image[c, lines] = running.astype(left_image.dtype)

    own = slice(0, 1), slice(0, vectors)
    others = slice(1, slots + 1), slice(vectors, columns)

    blank = overlap
    hits = [
        [[(place_ref[0, n, 0, o] == u).astype(jnp.int32) for o in range(overlap)] for n in range(slots)]
        for u in range(tiles)
    ]
    shift = [
        [sum((o - blank) * hits[u][n][o] for o in range(overlap)) for n in range(slots)]
        for u in range(tiles)
    ]
    for n in range(slots):
        for u in range(tiles):
            found_at[n * tiles + u] = first_of(n) + blank + shift[u][n]
    for k, offset in enumerate(OFFSETS):
        for i, u in enumerate(edges):
            spot = k * (overlap + 1) + blank
            for n in range(slots):
                spot = spot + (off_ref[n, s] == offset).astype(jnp.int32) * shift[u][n]
            rim_found_at[k * len(edges) + i] = spot

    group = bands - 1
    for first in range(0, tiles, group):
        for t in range(first, min(first + group, tiles)):
            stiff_copy(t).wait()
        for t in range(first, min(first + group, tiles)):
            if rim <= t < tiles - rim:
                image_of(t)
            left_of(t, *own)
    for c in range(tiles, tiles + 2 * rim):
        left_of(c, *own)
    wait_pair(own_copy)
    for t in edges:
        image_of(t)
    corner = None
    for t in range(tiles):
        term = dot_nt(basis[0, :, halo + t * rows : halo + (t + 1) * rows], image[t])
        corner = term if corner is None else corner + term
    part[0:vectors, 0:vectors] = corner

    for k in ARRIVALS:
        sub_copy(count - 1 - k, OFFSETS[count - 1 - k]).wait_recv()
        for i in range(len(edges)):
            tile = jnp.zeros((vectors, rows), arrived.dtype)
            for o in range(overlap):
                spot = k * (overlap + 1) + o
                tile = jnp.where(rim_found_at[k * len(edges) + i] == spot, arrived[spot], tile)
            lane = i % rim * rows
            rim_out[k, i // rim, :, lane : lane + rows] = tile
        if k != ARRIVALS[0]:
            start_pair(rim_copy(ARRIVALS[ARRIVALS.index(k) - 1]))
    for u in range(tiles):
        for n in range(slots):
            spot = halo + u * rows
            basis[n + 1, :, spot : spot + rows] = arrived[found_at[n * tiles + u]]
    start_pair(rim_copy(ARRIVALS[-1]))
    for c in range(tiles + 2 * rim):
        left_of(c, *others)
    for k in range(count):
        sub_copy(k, OFFSETS[k]).wait_send()

    for n in range(slots):
        low = below = None
        for o in range(overlap):
            tile = arrived[first_of(n) + o]
            spot = place_ref[0, n, 0, o]
            term = dot_nt(tile, image[spot])
            low = term if low is None else low + term
            term = dot_nt(left_image[rim + spot], tile)
            below = term if below is None else below + term
        lines = slice((n + 1) * vectors, (n + 2) * vectors)
        part[lines, 0:vectors] = low
        part[:, lines] = below

    def edge_partial(i):
        lane = i % rim * rows
        right = jnp.concatenate(
            [
                rim_in[off_ref[n, s] + RCH - (off_ref[n, s] > 0).astype(jnp.int32), i // rim, :, lane : lane + rows]
                for n in range(slots)
            ]
        )
        return dot_nt(left_image[i if i < rim else tiles + i], right)

    for k in range(count):
        wait_pair(rim_copy(k))
    sides = None
    for i in range(2 * rim):
        term = edge_partial(i)
        sides = term if sides is None else sides + term
    part[:, vectors:] += sides
    part_low[...] = part[...].astype(part_low.dtype)

    red_copies = []
    for step in range(1, layers):
        peer = lax.rem(g + step, layers)
        red_copies.append(
            pltpu.make_async_remote_copy(
                src_ref=part_low.at[pl.ds(pl.multiple_of(peer * share, share), share)],
                dst_ref=shares.at[step - 1],
                send_sem=red_send.at[step - 1],
                recv_sem=red_recv.at[step - 1],
                device_id=(s, peer),
                device_id_type=MESH,
            )
        )
    for copy in red_copies:
        copy.start()
    for copy in red_copies:
        copy.wait()
    result = part[pl.ds(pl.multiple_of(g * share, share), share), :]
    for step in range(1, layers):
        result = result + shares[step - 1].astype(jnp.float32)
    out_ref[0] = result


def on_device(subs, layers, stiffness, deflation, off_map, need_map, place_map):
    _, tiles, bands, rows, _ = stiffness.shape
    _, vectors, width = deflation.shape
    slots, overlap = place_map.shape[2:]
    columns = vectors * (slots + 1)
    halo = (bands // 2) * rows
    share = columns // layers
    count = len(OFFSETS)
    low = deflation.dtype
    dma = pltpu.SemaphoreType.DMA
    tables = (
        off_map.T,
        need_map.transpose(1, 2, 3, 0),
        place_map.transpose(0, 2, 1, 3),
    )
    return pl.pallas_call(
        functools.partial(kernel, subs, layers),
        out_shape=pltpu.VMEM((1, share, columns), jnp.float32),
        in_specs=[pl.BlockSpec(memory_space=pl.ANY)] * 5,
        out_specs=pl.BlockSpec(memory_space=pltpu.VMEM),
        scratch_shapes=[
            *[pltpu.SMEM(table.shape, table.dtype) for table in tables],
            pltpu.VMEM((tiles, bands, rows, rows), low),
            pltpu.VMEM((slots + 1, vectors, width + 2 * halo), low),
            pltpu.VMEM((tiles, vectors, rows), low),
            pltpu.VMEM((tiles + 2 * (bands // 2), columns, rows), low),
            pltpu.VMEM((tiles, vectors, rows), low),
            pltpu.VMEM((count, overlap, vectors, rows), low),
            pltpu.VMEM((count * (overlap + 1), vectors, rows), low),
            pltpu.VMEM((count, 2, vectors, halo), low),
            pltpu.VMEM((count, 2, vectors, halo), low),
            pltpu.SMEM((slots * tiles,), jnp.int32),
            pltpu.SMEM((count * 2 * (bands // 2),), jnp.int32),
            pltpu.VMEM((columns, columns), jnp.float32),
            pltpu.VMEM((columns, columns), low),
            pltpu.VMEM((layers - 1, share, columns), low),
            dma((4,)),
            dma((tiles,)),
            dma((count,)), dma((count,)),
            dma((2,)), dma((2,)),
            dma((count, 2)), dma((count, 2)),
            dma((layers - 1,)), dma((layers - 1,)),
        ],
        compiler_params=pltpu.CompilerParams(collective_id=0, has_side_effects=True),
    )(*tables, deflation, stiffness)


def solution(mesh):
    in_specs = (
        P("sub", "grp", None, None, None),
        P("sub", None, "grp"),
        P(),
        P(None, "grp", None, None),
        P("sub", "grp", None, None),
    )
    out_specs = P("sub", "grp", None)
    return jax.shard_map(
        functools.partial(on_device, mesh.shape["sub"], mesh.shape["grp"]),
        mesh=mesh,
        in_specs=in_specs,
        out_specs=out_specs,
        check_vma=False,
    )
```

```python
import functools

import jax
import jax.numpy as jnp
from jax import lax
from jax.experimental import pallas as pl
from jax.experimental.pallas import tpu as pltpu
from jax.sharding import PartitionSpec as P

RCH = 2
MESH = pl.DeviceIdType.MESH
OFFSETS = [value for value in range(-RCH, RCH + 1) if value != 0]
SEND_ORDER = sorted(OFFSETS, key=lambda value: (value < 0, abs(value)))
NEAR_FIRST = [1, 2, -2, -1]
ARRIVALS = [OFFSETS.index(-value) for value in SEND_ORDER]
NT = (((1,), (1,)), ((), ()))
NN = (((1,), (0,)), ((), ()))


def dot_nt(lhs, rhs):
    return lax.dot_general(lhs, rhs, NT, preferred_element_type=jnp.float32)


def dot_nn(lhs, rhs):
    return lax.dot_general(lhs, rhs, NN, preferred_element_type=jnp.float32)


def kernel(
    subs, layers, off_hbm, need_hbm, place_hbm, defl_ref, stiff_ref, out_ref,
    off_ref, need_ref, place_ref, a_buf, basis, image, left_image, own_tiles, outgoing, arrived,
    rim_out, rim_in, found_at, rim_found_at, part, part_low, shares,
    in_sem, a_sem, sub_send, sub_recv, own_send, own_recv, rim_send, rim_recv, red_send, red_recv,
):
    s = lax.axis_index("sub")
    g = lax.axis_index("grp")
    _, tiles, bands, rows, _ = stiff_ref.shape
    vectors = defl_ref.shape[1]
    slots = off_ref.shape[0]
    overlap = place_ref.shape[3]
    rim = bands // 2
    halo = rim * rows
    width = tiles * rows
    columns = vectors * (slots + 1)
    share = out_ref.shape[1]
    count = len(OFFSETS)
    has_left = g > 0
    has_right = g < layers - 1

    barrier = pltpu.get_barrier_semaphore()
    for offset in SEND_ORDER:
        pl.semaphore_signal(
            barrier, inc=1, device_id=(lax.rem(s + offset + subs, subs), g), device_id_type=MESH
        )
    for step in range(1, layers):
        pl.semaphore_signal(
            barrier, inc=1, device_id=(s, lax.rem(g + step, layers)), device_id_type=MESH
        )

    inputs = [
        pltpu.make_async_copy(off_hbm, off_ref, in_sem.at[0]),
        pltpu.make_async_copy(need_hbm, need_ref, in_sem.at[1]),
        pltpu.make_async_copy(place_hbm, place_ref, in_sem.at[2]),
        pltpu.make_async_copy(
            defl_ref.at[0], basis.at[0, :, pl.ds(halo, width)], in_sem.at[3]
        ),
    ]
    for copy in inputs:
        copy.start()

    def stiff_copy(t):
        return pltpu.make_async_copy(stiff_ref.at[0, t], a_buf.at[t], a_sem.at[t])

    edges = list(range(rim)) + list(range(tiles - rim, tiles))

    for k in range(count):
        arrived[k * (overlap + 1) + overlap] = jnp.zeros((vectors, rows), arrived.dtype)

    @pl.when(jnp.logical_not(has_left))
    def _():
        basis[0, :, 0:halo] = jnp.zeros((vectors, halo), basis.dtype)
        rim_in[:, 0] = jnp.zeros((count, vectors, halo), rim_in.dtype)

    @pl.when(jnp.logical_not(has_right))
    def _():
        basis[0, :, halo + width :] = jnp.zeros((vectors, halo), basis.dtype)
        rim_in[:, 1] = jnp.zeros((count, vectors, halo), rim_in.dtype)

    for copy in inputs:
        copy.wait()
    for t in range(tiles):
        stiff_copy(t).start()
    for u in range(tiles):
        own_tiles[u] = basis[0, :, halo + u * rows : halo + (u + 1) * rows]
    for k, offset in enumerate(OFFSETS):
        target = lax.rem(s + offset + subs, subs)
        for o in range(overlap):
            tile = jnp.int32(0)
            for n in range(slots):
                match = (off_ref[n, target] == -offset).astype(jnp.int32)
                tile = tile + match * need_ref[0, n, o, target]
            outgoing[k, o] = own_tiles[tile]

    pl.semaphore_wait(barrier, count + layers - 1)

    def sub_copy(k, offset):
        back = count - 1 - k
        return pltpu.make_async_remote_copy(
            src_ref=outgoing.at[k],
            dst_ref=arrived.at[pl.ds(back * (overlap + 1), overlap)],
            send_sem=sub_send.at[k],
            recv_sem=sub_recv.at[back],
            device_id=(lax.rem(s + offset + subs, subs), g),
            device_id_type=MESH,
        )

    lower = s < subs // 2
    for near, far in zip(NEAR_FIRST, SEND_ORDER):
        k, offset = OFFSETS.index(near), near
        if near != far:
            k = jnp.where(lower, k, OFFSETS.index(far))
            offset = jnp.where(lower, near, far)
        sub_copy(k, offset).start()

    def own_copy(to_left):
        source, target = (halo, halo + width) if to_left else (width, 0)
        return pltpu.make_async_remote_copy(
            src_ref=basis.at[0, :, pl.ds(source, halo)],
            dst_ref=basis.at[0, :, pl.ds(target, halo)],
            send_sem=own_send.at[0 if to_left else 1],
            recv_sem=own_recv.at[1 if to_left else 0],
            device_id=(s, g - 1 if to_left else g + 1),
            device_id_type=MESH,
        )

    def rim_copy(k):
        def make(to_left):
            source, target = (0, 1) if to_left else (1, 0)
            return pltpu.make_async_remote_copy(
                src_ref=rim_out.at[k, source],
                dst_ref=rim_in.at[k, target],
                send_sem=rim_send.at[k, 0 if to_left else 1],
                recv_sem=rim_recv.at[k, 1 if to_left else 0],
                device_id=(s, g - 1 if to_left else g + 1),
                device_id_type=MESH,
            )

        return make

    def start_pair(make):
        @pl.when(has_left)
        def _():
            make(True).start()

        @pl.when(has_right)
        def _():
            make(False).start()

    def wait_pair(make):
        @pl.when(has_left)
        def _():
            make(False).wait_recv()
            make(True).wait_send()

        @pl.when(has_right)
        def _():
            make(True).wait_recv()
            make(False).wait_send()

    start_pair(own_copy)

    def column(t):
        return t * rows if isinstance(t, int) else pl.multiple_of(t * rows, rows)

    def first_of(n):
        offset = off_ref[n, s]
        return (offset + RCH - (offset > 0).astype(jnp.int32)) * (overlap + 1)

    def image_of(t):
        running = None
        for b in range(bands):
            term = dot_nt(basis[0, :, pl.ds(column(t + b), rows)], a_buf[t, b])
            running = term if running is None else running + term
        image[t] = running.astype(image.dtype)

    def left_of(c, blocks, lines):
        running = None
        for b in range(bands):
            t = c - b
            if isinstance(t, int) and not 0 <= t < tiles:
                continue
            window = basis[blocks, :, pl.ds(column(t + rim), rows)]
            term = dot_nn(window.reshape(-1, rows), a_buf[t, b])
            running = term if running is None else running + term
        left_image[c, lines] = running.astype(left_image.dtype)

    own = slice(0, 1), slice(0, vectors)
    others = slice(1, slots + 1), slice(vectors, columns)

    blank = overlap
    hits = [
        [[(place_ref[0, n, 0, o] == u).astype(jnp.int32) for o in range(overlap)] for n in range(slots)]
        for u in range(tiles)
    ]
    shift = [
        [sum((o - blank) * hits[u][n][o] for o in range(overlap)) for n in range(slots)]
        for u in range(tiles)
    ]
    for n in range(slots):
        for u in range(tiles):
            found_at[n * tiles + u] = first_of(n) + blank + shift[u][n]
    for k, offset in enumerate(OFFSETS):
        for i, u in enumerate(edges):
            spot = k * (overlap + 1) + blank
            for n in range(slots):
                spot = spot + (off_ref[n, s] == offset).astype(jnp.int32) * shift[u][n]
            rim_found_at[k * len(edges) + i] = spot

    group = bands - 1
    for first in range(0, tiles, group):
        for t in range(first, min(first + group, tiles)):
            stiff_copy(t).wait()
        for t in range(first, min(first + group, tiles)):
            if rim <= t < tiles - rim:
                image_of(t)
            left_of(t, *own)
    for c in range(tiles, tiles + 2 * rim):
        left_of(c, *own)
    wait_pair(own_copy)
    for t in edges:
        image_of(t)
    def land(k):
        sub_copy(count - 1 - k, OFFSETS[count - 1 - k]).wait_recv()
        for i in range(len(edges)):
            tile = jnp.zeros((vectors, rows), arrived.dtype)
            for o in range(overlap):
                spot = k * (overlap + 1) + o
                tile = jnp.where(rim_found_at[k * len(edges) + i] == spot, arrived[spot], tile)
            lane = i % rim * rows
            rim_out[k, i // rim, :, lane : lane + rows] = tile

    def corner(first, last):
        total = None
        for t in range(first, last):
            term = dot_nt(basis[0, :, halo + t * rows : halo + (t + 1) * rows], image[t])
            total = term if total is None else total + term
        return total

    middle, early = tiles // 2, ARRIVALS[:2]
    for k in early:
        land(k)
    part[0:vectors, 0:vectors] = corner(0, middle)
    for k in early:
        start_pair(rim_copy(k))
    for k in ARRIVALS[2:-1]:
        land(k)
    part[0:vectors, 0:vectors] += corner(middle, tiles)
    for k in ARRIVALS[2:-1]:
        start_pair(rim_copy(k))
    land(ARRIVALS[-1])
    for u in range(tiles):
        for n in range(slots):
            spot = halo + u * rows
            basis[n + 1, :, spot : spot + rows] = arrived[found_at[n * tiles + u]]
    start_pair(rim_copy(ARRIVALS[-1]))
    for c in range(tiles + 2 * rim):
        left_of(c, *others)
    for k in range(count):
        sub_copy(k, OFFSETS[k]).wait_send()

    for n in range(slots):
        low = below = None
        for o in range(overlap):
            tile = arrived[first_of(n) + o]
            spot = place_ref[0, n, 0, o]
            term = dot_nt(tile, image[spot])
            low = term if low is None else low + term
            term = dot_nt(left_image[rim + spot], tile)
            below = term if below is None else below + term
        lines = slice((n + 1) * vectors, (n + 2) * vectors)
        part[lines, 0:vectors] = low
        part[:, lines] = below

    def edge_partial(i):
        lane = i % rim * rows
        right = jnp.concatenate(
            [
                rim_in[off_ref[n, s] + RCH - (off_ref[n, s] > 0).astype(jnp.int32), i // rim, :, lane : lane + rows]
                for n in range(slots)
            ]
        )
        return dot_nt(left_image[i if i < rim else tiles + i], right)

    for k in range(count):
        wait_pair(rim_copy(k))
    sides = None
    for i in range(2 * rim):
        term = edge_partial(i)
        sides = term if sides is None else sides + term
    part[:, vectors:] += sides
    part_low[...] = part[...].astype(part_low.dtype)

    red_copies = []
    for step in range(1, layers):
        peer = lax.rem(g + step, layers)
        red_copies.append(
            pltpu.make_async_remote_copy(
                src_ref=part_low.at[pl.ds(pl.multiple_of(peer * share, share), share)],
                dst_ref=shares.at[step - 1],
                send_sem=red_send.at[step - 1],
                recv_sem=red_recv.at[step - 1],
                device_id=(s, peer),
                device_id_type=MESH,
            )
        )
    for copy in red_copies:
        copy.start()
    for copy in red_copies:
        copy.wait()
    result = part[pl.ds(pl.multiple_of(g * share, share), share), :]
    for step in range(1, layers):
        result = result + shares[step - 1].astype(jnp.float32)
    out_ref[0] = result


def on_device(subs, layers, stiffness, deflation, off_map, need_map, place_map):
    _, tiles, bands, rows, _ = stiffness.shape
    _, vectors, width = deflation.shape
    slots, overlap = place_map.shape[2:]
    columns = vectors * (slots + 1)
    halo = (bands // 2) * rows
    share = columns // layers
    count = len(OFFSETS)
    low = deflation.dtype
    dma = pltpu.SemaphoreType.DMA
    tables = (
        off_map.T,
        need_map.transpose(1, 2, 3, 0),
        place_map.transpose(0, 2, 1, 3),
    )
    return pl.pallas_call(
        functools.partial(kernel, subs, layers),
        out_shape=pltpu.VMEM((1, share, columns), jnp.float32),
        in_specs=[pl.BlockSpec(memory_space=pl.ANY)] * 5,
        out_specs=pl.BlockSpec(memory_space=pltpu.VMEM),
        scratch_shapes=[
            *[pltpu.SMEM(table.shape, table.dtype) for table in tables],
            pltpu.VMEM((tiles, bands, rows, rows), low),
            pltpu.VMEM((slots + 1, vectors, width + 2 * halo), low),
            pltpu.VMEM((tiles, vectors, rows), low),
            pltpu.VMEM((tiles + 2 * (bands // 2), columns, rows), low),
            pltpu.VMEM((tiles, vectors, rows), low),
            pltpu.VMEM((count, overlap, vectors, rows), low),
            pltpu.VMEM((count * (overlap + 1), vectors, rows), low),
            pltpu.VMEM((count, 2, vectors, halo), low),
            pltpu.VMEM((count, 2, vectors, halo), low),
            pltpu.SMEM((slots * tiles,), jnp.int32),
            pltpu.SMEM((count * 2 * (bands // 2),), jnp.int32),
            pltpu.VMEM((columns, columns), jnp.float32),
            pltpu.VMEM((columns, columns), low),
            pltpu.VMEM((layers - 1, share, columns), low),
            dma((4,)),
            dma((tiles,)),
            dma((count,)), dma((count,)),
            dma((2,)), dma((2,)),
            dma((count, 2)), dma((count, 2)),
            dma((layers - 1,)), dma((layers - 1,)),
        ],
        compiler_params=pltpu.CompilerParams(collective_id=0, has_side_effects=True),
    )(*tables, deflation, stiffness)


def solution(mesh):
    in_specs = (
        P("sub", "grp", None, None, None),
        P("sub", None, "grp"),
        P(),
        P(None, "grp", None, None),
        P("sub", "grp", None, None),
    )
    out_specs = P("sub", "grp", None)
    return jax.shard_map(
        functools.partial(on_device, mesh.shape["sub"], mesh.shape["grp"]),
        mesh=mesh,
        in_specs=in_specs,
        out_specs=out_specs,
        check_vma=False,
    )
```

```python
import functools

import jax
import jax.numpy as jnp
from jax import lax
from jax.experimental import pallas as pl
from jax.experimental.pallas import tpu as pltpu
from jax.sharding import PartitionSpec as P

RCH = 2
MESH = pl.DeviceIdType.MESH
OFFSETS = [value for value in range(-RCH, RCH + 1) if value != 0]
SEND_ORDER = sorted(OFFSETS, key=lambda value: (value < 0, abs(value)))
NEAR_FIRST = [1, 2, -2, -1]
NT = (((1,), (1,)), ((), ()))
NN = (((1,), (0,)), ((), ()))


def dot_nt(lhs, rhs):
    return lax.dot_general(lhs, rhs, NT, preferred_element_type=jnp.float32)


def dot_nn(lhs, rhs):
    return lax.dot_general(lhs, rhs, NN, preferred_element_type=jnp.float32)


def kernel(
    subs, layers, off_hbm, need_hbm, place_hbm, defl_ref, stiff_ref, out_ref,
    off_ref, need_ref, place_ref, a_buf, basis, image, left_image, own_tiles, outgoing, arrived,
    products, rim_out, rim_in, found_at, rim_found_at, spot_at, part, part_low, shares,
    in_sem, a_sem, sub_send, sub_recv, own_send, own_recv, rim_send, rim_recv, red_send, red_recv,
):
    s = lax.axis_index("sub")
    g = lax.axis_index("grp")
    _, tiles, bands, rows, _ = stiff_ref.shape
    vectors = defl_ref.shape[1]
    slots = off_ref.shape[0]
    overlap = place_ref.shape[3]
    rim = bands // 2
    halo = rim * rows
    width = tiles * rows
    columns = vectors * (slots + 1)
    share = out_ref.shape[1]
    count = len(OFFSETS)
    has_left = g > 0
    has_right = g < layers - 1

    barrier = pltpu.get_barrier_semaphore()
    for offset in SEND_ORDER:
        pl.semaphore_signal(
            barrier, inc=1, device_id=(lax.rem(s + offset + subs, subs), g), device_id_type=MESH
        )
    for step in range(1, layers):
        pl.semaphore_signal(
            barrier, inc=1, device_id=(s, lax.rem(g + step, layers)), device_id_type=MESH
        )

    inputs = [
        pltpu.make_async_copy(off_hbm, off_ref, in_sem.at[0]),
        pltpu.make_async_copy(need_hbm, need_ref, in_sem.at[1]),
        pltpu.make_async_copy(place_hbm, place_ref, in_sem.at[2]),
        pltpu.make_async_copy(
            defl_ref.at[0], basis.at[0, :, pl.ds(halo, width)], in_sem.at[3]
        ),
    ]
    for copy in inputs:
        copy.start()

    def stiff_copy(t):
        return pltpu.make_async_copy(stiff_ref.at[0, t], a_buf.at[t], a_sem.at[t])

    edges = list(range(rim)) + list(range(tiles - rim, tiles))

    for k in range(count):
        products[k * (overlap + 1) + overlap] = jnp.zeros((bands, vectors, rows), products.dtype)

    @pl.when(jnp.logical_not(has_left))
    def _():
        basis[0, :, 0:halo] = jnp.zeros((vectors, halo), basis.dtype)
        rim_in[:, 0] = jnp.zeros((count, vectors, halo), rim_in.dtype)

    @pl.when(jnp.logical_not(has_right))
    def _():
        basis[0, :, halo + width :] = jnp.zeros((vectors, halo), basis.dtype)
        rim_in[:, 1] = jnp.zeros((count, vectors, halo), rim_in.dtype)

    for copy in inputs:
        copy.wait()
    for t in range(tiles):
        stiff_copy(t).start()
    for u in range(tiles):
        own_tiles[u] = basis[0, :, halo + u * rows : halo + (u + 1) * rows]
    for k, offset in enumerate(OFFSETS):
        target = lax.rem(s + offset + subs, subs)
        for o in range(overlap):
            tile = jnp.int32(0)
            for n in range(slots):
                match = (off_ref[n, target] == -offset).astype(jnp.int32)
                tile = tile + match * need_ref[0, n, o, target]
            outgoing[k, o] = own_tiles[tile]

    pl.semaphore_wait(barrier, count + layers - 1)

    def sub_copy(k, offset):
        back = count - 1 - k
        return pltpu.make_async_remote_copy(
            src_ref=outgoing.at[k],
            dst_ref=arrived.at[pl.ds(back * (overlap + 1), overlap)],
            send_sem=sub_send.at[k],
            recv_sem=sub_recv.at[back],
            device_id=(lax.rem(s + offset + subs, subs), g),
            device_id_type=MESH,
        )

    lower = s < subs // 2
    for near, far in zip(NEAR_FIRST, SEND_ORDER):
        k, offset = OFFSETS.index(near), near
        if near != far:
            k = jnp.where(lower, k, OFFSETS.index(far))
            offset = jnp.where(lower, near, far)
        sub_copy(k, offset).start()

    def own_copy(to_left):
        source, target = (halo, halo + width) if to_left else (width, 0)
        return pltpu.make_async_remote_copy(
            src_ref=basis.at[0, :, pl.ds(source, halo)],
            dst_ref=basis.at[0, :, pl.ds(target, halo)],
            send_sem=own_send.at[0 if to_left else 1],
            recv_sem=own_recv.at[1 if to_left else 0],
            device_id=(s, g - 1 if to_left else g + 1),
            device_id_type=MESH,
        )

    def rim_copy(k):
        def make(to_left):
            source, target = (0, 1) if to_left else (1, 0)
            return pltpu.make_async_remote_copy(
                src_ref=rim_out.at[k, source],
                dst_ref=rim_in.at[k, target],
                send_sem=rim_send.at[k, 0 if to_left else 1],
                recv_sem=rim_recv.at[k, 1 if to_left else 0],
                device_id=(s, g - 1 if to_left else g + 1),
                device_id_type=MESH,
            )

        return make

    def start_pair(make):
        @pl.when(has_left)
        def _():
            make(True).start()

        @pl.when(has_right)
        def _():
            make(False).start()

    def wait_pair(make):
        @pl.when(has_left)
        def _():
            make(False).wait_recv()
            make(True).wait_send()

        @pl.when(has_right)
        def _():
            make(True).wait_recv()
            make(False).wait_send()

    start_pair(own_copy)

    def column(t):
        return t * rows if isinstance(t, int) else pl.multiple_of(t * rows, rows)

    def first_of(n):
        offset = off_ref[n, s]
        return (offset + RCH - (offset > 0).astype(jnp.int32)) * (overlap + 1)

    def image_of(t):
        running = None
        for b in range(bands):
            term = dot_nt(basis[0, :, pl.ds(column(t + b), rows)], a_buf[t, b])
            running = term if running is None else running + term
        image[t] = running.astype(image.dtype)

    def left_of(c):
        running = None
        for b in range(bands):
            t = c - b
            if not 0 <= t < tiles:
                continue
            term = dot_nn(basis[0, :, (t + rim) * rows : (t + rim + 1) * rows], a_buf[t, b])
            running = term if running is None else running + term
        left_image[c, 0:vectors] = running.astype(left_image.dtype)

    blank = overlap
    hits = [
        [[(place_ref[0, n, 0, o] == u).astype(jnp.int32) for o in range(overlap)] for n in range(slots)]
        for u in range(tiles)
    ]
    shift = [
        [sum((o - blank) * hits[u][n][o] for o in range(overlap)) for n in range(slots)]
        for u in range(tiles)
    ]
    for n in range(slots):
        for u in range(tiles):
            found_at[n * tiles + u] = first_of(n) + blank + shift[u][n]
    for k, offset in enumerate(OFFSETS):
        for i, u in enumerate(edges):
            spot = k * (overlap + 1) + blank
            for n in range(slots):
                spot = spot + (off_ref[n, s] == offset).astype(jnp.int32) * shift[u][n]
            rim_found_at[k * len(edges) + i] = spot
        for o in range(overlap):
            spot = jnp.int32(0)
            for n in range(slots):
                spot = spot + (off_ref[n, s] == offset).astype(jnp.int32) * place_ref[0, n, 0, o]
            spot_at[k * overlap + o] = spot

    group = bands - 1
    for first in range(0, tiles, group):
        for t in range(first, min(first + group, tiles)):
            stiff_copy(t).wait()
        for t in range(first, min(first + group, tiles)):
            if rim <= t < tiles - rim:
                image_of(t)
            left_of(t)
    for c in range(tiles, tiles + 2 * rim):
        left_of(c)
    wait_pair(own_copy)
    for t in edges:
        image_of(t)
    corner = None
    for t in range(tiles):
        term = dot_nt(basis[0, :, halo + t * rows : halo + (t + 1) * rows], image[t])
        corner = term if corner is None else corner + term
    part[0:vectors, 0:vectors] = corner

    def land(k):
        sent = count - 1 - k
        if isinstance(k, int):
            offset = OFFSETS[sent]
        else:
            offset = sent - RCH + (sent >= RCH).astype(jnp.int32)
        sub_copy(sent, offset).wait_recv()
        for i in range(len(edges)):
            tile = jnp.zeros((vectors, rows), arrived.dtype)
            for o in range(overlap):
                hit = rim_found_at[k * len(edges) + i] == k * (overlap + 1) + o
                tile = jnp.where(hit, arrived[k * (overlap + 1) + o], tile)
            lane = i % rim * rows
            rim_out[k, i // rim, :, lane : lane + rows] = tile
        for o in range(overlap):
            spot = spot_at[k * overlap + o]
            for b in range(bands):
                term = dot_nn(arrived[k * (overlap + 1) + o], a_buf[spot, b])
                products[k * (overlap + 1) + o, b] = term.astype(products.dtype)
            if o == 0:
                start_pair(rim_copy(k))

    low_end, high_end = s == RCH - 1, s == subs - 1
    land(1)
    land(jnp.where(low_end, 2, 0))
    land(jnp.where(jnp.logical_or(low_end, high_end), 3, 2))
    land(jnp.where(low_end, 0, jnp.where(high_end, 2, 3)))
    for c in range(tiles + 2 * rim):
        for n in range(slots):
            total = None
            for b in range(bands):
                t = c - b
                if 0 <= t < tiles:
                    term = products[found_at[n * tiles + t], b]
                    total = term if total is None else total + term
            left_image[c, (n + 1) * vectors : (n + 2) * vectors] = total
    for k in range(count):
        sub_copy(k, OFFSETS[k]).wait_send()

    for n in range(slots):
        low = below = None
        for o in range(overlap):
            tile = arrived[first_of(n) + o]
            spot = place_ref[0, n, 0, o]
            term = dot_nt(tile, image[spot])
            low = term if low is None else low + term
            term = dot_nt(left_image[rim + spot], tile)
            below = term if below is None else below + term
        lines = slice((n + 1) * vectors, (n + 2) * vectors)
        part[lines, 0:vectors] = low
        part[:, lines] = below

    def edge_partial(i):
        lane = i % rim * rows
        right = jnp.concatenate(
            [
                rim_in[off_ref[n, s] + RCH - (off_ref[n, s] > 0).astype(jnp.int32), i // rim, :, lane : lane + rows]
                for n in range(slots)
            ]
        )
        return dot_nt(left_image[i if i < rim else tiles + i], right)

    for k in range(count):
        wait_pair(rim_copy(k))
    sides = None
    for i in range(2 * rim):
        term = edge_partial(i)
        sides = term if sides is None else sides + term
    part[:, vectors:] += sides
    part_low[...] = part[...].astype(part_low.dtype)

    red_copies = []
    for step in range(1, layers):
        peer = lax.rem(g + step, layers)
        red_copies.append(
            pltpu.make_async_remote_copy(
                src_ref=part_low.at[pl.ds(pl.multiple_of(peer * share, share), share)],
                dst_ref=shares.at[step - 1],
                send_sem=red_send.at[step - 1],
                recv_sem=red_recv.at[step - 1],
                device_id=(s, peer),
                device_id_type=MESH,
            )
        )
    for copy in red_copies:
        copy.start()
    for copy in red_copies:
        copy.wait()
    result = part[pl.ds(pl.multiple_of(g * share, share), share), :]
    for step in range(1, layers):
        result = result + shares[step - 1].astype(jnp.float32)
    out_ref[0] = result


def on_device(subs, layers, stiffness, deflation, off_map, need_map, place_map):
    _, tiles, bands, rows, _ = stiffness.shape
    _, vectors, width = deflation.shape
    slots, overlap = place_map.shape[2:]
    columns = vectors * (slots + 1)
    halo = (bands // 2) * rows
    share = columns // layers
    count = len(OFFSETS)
    low = deflation.dtype
    dma = pltpu.SemaphoreType.DMA
    tables = (
        off_map.T,
        need_map.transpose(1, 2, 3, 0),
        place_map.transpose(0, 2, 1, 3),
    )
    return pl.pallas_call(
        functools.partial(kernel, subs, layers),
        out_shape=pltpu.VMEM((1, share, columns), jnp.float32),
        in_specs=[pl.BlockSpec(memory_space=pl.ANY)] * 5,
        out_specs=pl.BlockSpec(memory_space=pltpu.VMEM),
        scratch_shapes=[
            *[pltpu.SMEM(table.shape, table.dtype) for table in tables],
            pltpu.VMEM((tiles, bands, rows, rows), low),
            pltpu.VMEM((1, vectors, width + 2 * halo), low),
            pltpu.VMEM((tiles, vectors, rows), low),
            pltpu.VMEM((tiles + 2 * (bands // 2), columns, rows), low),
            pltpu.VMEM((tiles, vectors, rows), low),
            pltpu.VMEM((count, overlap, vectors, rows), low),
            pltpu.VMEM((count * (overlap + 1), vectors, rows), low),
            pltpu.VMEM((count * (overlap + 1), bands, vectors, rows), low),
            pltpu.VMEM((count, 2, vectors, halo), low),
            pltpu.VMEM((count, 2, vectors, halo), low),
            pltpu.SMEM((slots * tiles,), jnp.int32),
            pltpu.SMEM((count * 2 * (bands // 2),), jnp.int32),
            pltpu.SMEM((count * overlap,), jnp.int32),
            pltpu.VMEM((columns, columns), jnp.float32),
            pltpu.VMEM((columns, columns), low),
            pltpu.VMEM((layers - 1, share, columns), low),
            dma((4,)),
            dma((tiles,)),
            dma((count,)), dma((count,)),
            dma((2,)), dma((2,)),
            dma((count, 2)), dma((count, 2)),
            dma((layers - 1,)), dma((layers - 1,)),
        ],
        compiler_params=pltpu.CompilerParams(collective_id=0, has_side_effects=True),
    )(*tables, deflation, stiffness)


def solution(mesh):
    in_specs = (
        P("sub", "grp", None, None, None),
        P("sub", None, "grp"),
        P(),
        P(None, "grp", None, None),
        P("sub", "grp", None, None),
    )
    out_specs = P("sub", "grp", None)
    return jax.shard_map(
        functools.partial(on_device, mesh.shape["sub"], mesh.shape["grp"]),
        mesh=mesh,
        in_specs=in_specs,
        out_specs=out_specs,
        check_vma=False,
    )
```

```python
import functools

import jax
import jax.numpy as jnp
from jax import lax
from jax.experimental import pallas as pl
from jax.experimental.pallas import tpu as pltpu
from jax.sharding import PartitionSpec as P

RCH = 2
MESH = pl.DeviceIdType.MESH
OFFSETS = [value for value in range(-RCH, RCH + 1) if value != 0]
SEND_ORDER = sorted(OFFSETS, key=lambda value: (value < 0, abs(value)))
NEAR_FIRST = [1, 2, -2, -1]
NT = (((1,), (1,)), ((), ()))
NN = (((1,), (0,)), ((), ()))


def dot_nt(lhs, rhs):
    return lax.dot_general(lhs, rhs, NT, preferred_element_type=jnp.float32)


def dot_nn(lhs, rhs):
    return lax.dot_general(lhs, rhs, NN, preferred_element_type=jnp.float32)


def kernel(
    subs, layers, off_hbm, need_hbm, place_hbm, defl_ref, stiff_ref, out_ref,
    off_ref, need_ref, place_ref, a_buf, basis, image, left_image, own_tiles, outgoing, arrived,
    products, rim_out, rim_in, found_at, rim_found_at, spot_at, part, part_low, shares,
    in_sem, a_sem, sub_send, sub_recv, own_send, own_recv, rim_send, rim_recv, red_send, red_recv,
):
    s = lax.axis_index("sub")
    g = lax.axis_index("grp")
    _, tiles, bands, rows, _ = stiff_ref.shape
    vectors = defl_ref.shape[1]
    slots = off_ref.shape[0]
    overlap = place_ref.shape[3]
    rim = bands // 2
    halo = rim * rows
    width = tiles * rows
    columns = vectors * (slots + 1)
    share = out_ref.shape[1]
    count = len(OFFSETS)
    has_left = g > 0
    has_right = g < layers - 1

    barrier = pltpu.get_barrier_semaphore()
    for offset in SEND_ORDER:
        pl.semaphore_signal(
            barrier, inc=1, device_id=(lax.rem(s + offset + subs, subs), g), device_id_type=MESH
        )
    for step in range(1, layers):
        pl.semaphore_signal(
            barrier, inc=1, device_id=(s, lax.rem(g + step, layers)), device_id_type=MESH
        )

    inputs = [
        pltpu.make_async_copy(off_hbm, off_ref, in_sem.at[0]),
        pltpu.make_async_copy(need_hbm, need_ref, in_sem.at[1]),
        pltpu.make_async_copy(place_hbm, place_ref, in_sem.at[2]),
        pltpu.make_async_copy(
            defl_ref.at[0], basis.at[0, :, pl.ds(halo, width)], in_sem.at[3]
        ),
    ]
    for copy in inputs:
        copy.start()

    def stiff_copy(t):
        return pltpu.make_async_copy(stiff_ref.at[0, t], a_buf.at[t], a_sem.at[t])

    edges = list(range(rim)) + list(range(tiles - rim, tiles))

    for k in range(count):
        products[k * (overlap + 1) + overlap] = jnp.zeros((bands, vectors, rows), products.dtype)

    @pl.when(jnp.logical_not(has_left))
    def _():
        basis[0, :, 0:halo] = jnp.zeros((vectors, halo), basis.dtype)
        rim_in[:, 0] = jnp.zeros((count, vectors, halo), rim_in.dtype)

    @pl.when(jnp.logical_not(has_right))
    def _():
        basis[0, :, halo + width :] = jnp.zeros((vectors, halo), basis.dtype)
        rim_in[:, 1] = jnp.zeros((count, vectors, halo), rim_in.dtype)

    for copy in inputs:
        copy.wait()
    for t in range(tiles):
        stiff_copy(t).start()
    for u in range(tiles):
        own_tiles[u] = basis[0, :, halo + u * rows : halo + (u + 1) * rows]
    for k, offset in enumerate(OFFSETS):
        target = lax.rem(s + offset + subs, subs)
        for o in range(overlap):
            tile = jnp.int32(0)
            for n in range(slots):
                match = (off_ref[n, target] == -offset).astype(jnp.int32)
                tile = tile + match * need_ref[0, n, o, target]
            outgoing[k, o] = own_tiles[tile]

    def column(t):
        return t * rows if isinstance(t, int) else pl.multiple_of(t * rows, rows)

    def image_of(t):
        running = None
        for b in range(bands):
            term = dot_nt(basis[0, :, pl.ds(column(t + b), rows)], a_buf[t, b])
            running = term if running is None else running + term
        image[t] = running.astype(image.dtype)

    def left_of(c):
        running = None
        for b in range(bands):
            t = c - b
            if not 0 <= t < tiles:
                continue
            term = dot_nn(basis[0, :, (t + rim) * rows : (t + rim + 1) * rows], a_buf[t, b])
            running = term if running is None else running + term
        left_image[c, 0:vectors] = running.astype(left_image.dtype)

    group = bands - 1
    ahead = tiles // 2 // group * group
    waits_long = s < RCH - 1

    def own_tiles_from(start, stop):
        for first in range(start, stop, group):
            for t in range(first, min(first + group, stop)):
                stiff_copy(t).wait()
            for t in range(first, min(first + group, stop)):
                if rim <= t < tiles - rim:
                    image_of(t)
                left_of(t)

    @pl.when(waits_long)
    def _():
        own_tiles_from(0, ahead)

    pl.semaphore_wait(barrier, count + layers - 1)

    def sub_copy(k, offset):
        back = count - 1 - k
        return pltpu.make_async_remote_copy(
            src_ref=outgoing.at[k],
            dst_ref=arrived.at[pl.ds(back * (overlap + 1), overlap)],
            send_sem=sub_send.at[k],
            recv_sem=sub_recv.at[back],
            device_id=(lax.rem(s + offset + subs, subs), g),
            device_id_type=MESH,
        )

    lower = s < subs // 2
    for near, far in zip(NEAR_FIRST, SEND_ORDER):
        k, offset = OFFSETS.index(near), near
        if near != far:
            k = jnp.where(lower, k, OFFSETS.index(far))
            offset = jnp.where(lower, near, far)
        sub_copy(k, offset).start()

    def own_copy(to_left):
        source, target = (halo, halo + width) if to_left else (width, 0)
        return pltpu.make_async_remote_copy(
            src_ref=basis.at[0, :, pl.ds(source, halo)],
            dst_ref=basis.at[0, :, pl.ds(target, halo)],
            send_sem=own_send.at[0 if to_left else 1],
            recv_sem=own_recv.at[1 if to_left else 0],
            device_id=(s, g - 1 if to_left else g + 1),
            device_id_type=MESH,
        )

    def rim_copy(k):
        def make(to_left):
            source, target = (0, 1) if to_left else (1, 0)
            return pltpu.make_async_remote_copy(
                src_ref=rim_out.at[k, source],
                dst_ref=rim_in.at[k, target],
                send_sem=rim_send.at[k, 0 if to_left else 1],
                recv_sem=rim_recv.at[k, 1 if to_left else 0],
                device_id=(s, g - 1 if to_left else g + 1),
                device_id_type=MESH,
            )

        return make

    def start_pair(make):
        @pl.when(has_left)
        def _():
            make(True).start()

        @pl.when(has_right)
        def _():
            make(False).start()

    def wait_pair(make):
        @pl.when(has_left)
        def _():
            make(False).wait_recv()
            make(True).wait_send()

        @pl.when(has_right)
        def _():
            make(True).wait_recv()
            make(False).wait_send()

    start_pair(own_copy)

    def first_of(n):
        offset = off_ref[n, s]
        return (offset + RCH - (offset > 0).astype(jnp.int32)) * (overlap + 1)

    blank = overlap
    hits = [
        [[(place_ref[0, n, 0, o] == u).astype(jnp.int32) for o in range(overlap)] for n in range(slots)]
        for u in range(tiles)
    ]
    shift = [
        [sum((o - blank) * hits[u][n][o] for o in range(overlap)) for n in range(slots)]
        for u in range(tiles)
    ]
    for n in range(slots):
        for u in range(tiles):
            found_at[n * tiles + u] = first_of(n) + blank + shift[u][n]
    for k, offset in enumerate(OFFSETS):
        for i, u in enumerate(edges):
            spot = k * (overlap + 1) + blank
            for n in range(slots):
                spot = spot + (off_ref[n, s] == offset).astype(jnp.int32) * shift[u][n]
            rim_found_at[k * len(edges) + i] = spot
        for o in range(overlap):
            spot = jnp.int32(0)
            for n in range(slots):
                spot = spot + (off_ref[n, s] == offset).astype(jnp.int32) * place_ref[0, n, 0, o]
            spot_at[k * overlap + o] = spot

    @pl.when(jnp.logical_not(waits_long))
    def _():
        own_tiles_from(0, ahead)

    own_tiles_from(ahead, tiles)
    for c in range(tiles, tiles + 2 * rim):
        left_of(c)
    wait_pair(own_copy)
    for t in edges:
        image_of(t)
    corner = None
    for t in range(tiles):
        term = dot_nt(basis[0, :, halo + t * rows : halo + (t + 1) * rows], image[t])
        corner = term if corner is None else corner + term
    part[0:vectors, 0:vectors] = corner

    def land(k):
        sent = count - 1 - k
        if isinstance(k, int):
            offset = OFFSETS[sent]
        else:
            offset = sent - RCH + (sent >= RCH).astype(jnp.int32)
        sub_copy(sent, offset).wait_recv()
        for i in range(len(edges)):
            tile = jnp.zeros((vectors, rows), arrived.dtype)
            for o in range(overlap):
                hit = rim_found_at[k * len(edges) + i] == k * (overlap + 1) + o
                tile = jnp.where(hit, arrived[k * (overlap + 1) + o], tile)
            lane = i % rim * rows
            rim_out[k, i // rim, :, lane : lane + rows] = tile
        for o in range(overlap):
            spot = spot_at[k * overlap + o]
            for b in range(bands):
                term = dot_nn(arrived[k * (overlap + 1) + o], a_buf[spot, b])
                products[k * (overlap + 1) + o, b] = term.astype(products.dtype)
            if o == 0:
                start_pair(rim_copy(k))

    low_end, high_end = s == RCH - 1, s == subs - 1
    land(1)
    land(jnp.where(low_end, 3, 0))
    land(jnp.where(low_end, 0, jnp.where(high_end, 3, 2)))
    land(jnp.where(jnp.logical_or(low_end, high_end), 2, 3))
    for c in range(tiles + 2 * rim):
        for n in range(slots):
            total = None
            for b in range(bands):
                t = c - b
                if 0 <= t < tiles:
                    term = products[found_at[n * tiles + t], b]
                    total = term if total is None else total + term
            left_image[c, (n + 1) * vectors : (n + 2) * vectors] = total
    for k in range(count):
        sub_copy(k, OFFSETS[k]).wait_send()

    for n in range(slots):
        low = below = None
        for o in range(overlap):
            tile = arrived[first_of(n) + o]
            spot = place_ref[0, n, 0, o]
            term = dot_nt(tile, image[spot])
            low = term if low is None else low + term
            term = dot_nt(left_image[rim + spot], tile)
            below = term if below is None else below + term
        lines = slice((n + 1) * vectors, (n + 2) * vectors)
        part[lines, 0:vectors] = low
        part[:, lines] = below

    def edge_partial(i):
        lane = i % rim * rows
        right = jnp.concatenate(
            [
                rim_in[off_ref[n, s] + RCH - (off_ref[n, s] > 0).astype(jnp.int32), i // rim, :, lane : lane + rows]
                for n in range(slots)
            ]
        )
        return dot_nt(left_image[i if i < rim else tiles + i], right)

    for k in range(count):
        wait_pair(rim_copy(k))
    sides = None
    for i in range(2 * rim):
        term = edge_partial(i)
        sides = term if sides is None else sides + term
    part[:, vectors:] += sides
    part_low[...] = part[...].astype(part_low.dtype)

    red_copies = []
    for step in range(1, layers):
        peer = lax.rem(g + step, layers)
        red_copies.append(
            pltpu.make_async_remote_copy(
                src_ref=part_low.at[pl.ds(pl.multiple_of(peer * share, share), share)],
                dst_ref=shares.at[step - 1],
                send_sem=red_send.at[step - 1],
                recv_sem=red_recv.at[step - 1],
                device_id=(s, peer),
                device_id_type=MESH,
            )
        )
    for copy in red_copies:
        copy.start()
    for copy in red_copies:
        copy.wait()
    result = part[pl.ds(pl.multiple_of(g * share, share), share), :]
    for step in range(1, layers):
        result = result + shares[step - 1].astype(jnp.float32)
    out_ref[0] = result


def on_device(subs, layers, stiffness, deflation, off_map, need_map, place_map):
    _, tiles, bands, rows, _ = stiffness.shape
    _, vectors, width = deflation.shape
    slots, overlap = place_map.shape[2:]
    columns = vectors * (slots + 1)
    halo = (bands // 2) * rows
    share = columns // layers
    count = len(OFFSETS)
    low = deflation.dtype
    dma = pltpu.SemaphoreType.DMA
    tables = (
        off_map.T,
        need_map.transpose(1, 2, 3, 0),
        place_map.transpose(0, 2, 1, 3),
    )
    return pl.pallas_call(
        functools.partial(kernel, subs, layers),
        out_shape=pltpu.VMEM((1, share, columns), jnp.float32),
        in_specs=[pl.BlockSpec(memory_space=pl.ANY)] * 5,
        out_specs=pl.BlockSpec(memory_space=pltpu.VMEM),
        scratch_shapes=[
            *[pltpu.SMEM(table.shape, table.dtype) for table in tables],
            pltpu.VMEM((tiles, bands, rows, rows), low),
            pltpu.VMEM((1, vectors, width + 2 * halo), low),
            pltpu.VMEM((tiles, vectors, rows), low),
            pltpu.VMEM((tiles + 2 * (bands // 2), columns, rows), low),
            pltpu.VMEM((tiles, vectors, rows), low),
            pltpu.VMEM((count, overlap, vectors, rows), low),
            pltpu.VMEM((count * (overlap + 1), vectors, rows), low),
            pltpu.VMEM((count * (overlap + 1), bands, vectors, rows), low),
            pltpu.VMEM((count, 2, vectors, halo), low),
            pltpu.VMEM((count, 2, vectors, halo), low),
            pltpu.SMEM((slots * tiles,), jnp.int32),
            pltpu.SMEM((count * 2 * (bands // 2),), jnp.int32),
            pltpu.SMEM((count * overlap,), jnp.int32),
            pltpu.VMEM((columns, columns), jnp.float32),
            pltpu.VMEM((columns, columns), low),
            pltpu.VMEM((layers - 1, share, columns), low),
            dma((4,)),
            dma((tiles,)),
            dma((count,)), dma((count,)),
            dma((2,)), dma((2,)),
            dma((count, 2)), dma((count, 2)),
            dma((layers - 1,)), dma((layers - 1,)),
        ],
        compiler_params=pltpu.CompilerParams(collective_id=0, has_side_effects=True),
    )(*tables, deflation, stiffness)


def solution(mesh):
    in_specs = (
        P("sub", "grp", None, None, None),
        P("sub", None, "grp"),
        P(),
        P(None, "grp", None, None),
        P("sub", "grp", None, None),
    )
    out_specs = P("sub", "grp", None)
    return jax.shard_map(
        functools.partial(on_device, mesh.shape["sub"], mesh.shape["grp"]),
        mesh=mesh,
        in_specs=in_specs,
        out_specs=out_specs,
        check_vma=False,
    )
```

```python
import functools

import jax
import jax.numpy as jnp
from jax import lax
from jax.experimental import pallas as pl
from jax.experimental.pallas import tpu as pltpu
from jax.sharding import PartitionSpec as P

RCH = 2
MESH = pl.DeviceIdType.MESH
OFFSETS = [value for value in range(-RCH, RCH + 1) if value != 0]
SEND_ORDER = sorted(OFFSETS, key=lambda value: (value < 0, abs(value)))
NEAR_FIRST = [1, 2, -2, -1]
NT = (((1,), (1,)), ((), ()))
NN = (((1,), (0,)), ((), ()))


def dot_nt(lhs, rhs):
    return lax.dot_general(lhs, rhs, NT, preferred_element_type=jnp.float32)


def dot_nn(lhs, rhs):
    return lax.dot_general(lhs, rhs, NN, preferred_element_type=jnp.float32)


def kernel(
    subs, layers, off_hbm, need_hbm, place_hbm, defl_ref, stiff_ref, out_ref,
    off_ref, need_ref, place_ref, a_buf, basis, image, left_image, own_tiles, outgoing, arrived,
    products, rim_out, rim_in, found_at, rim_found_at, spot_at, part, part_low, shares,
    in_sem, a_sem, sub_send, sub_recv, own_send, own_recv, rim_send, rim_recv, red_send, red_recv,
):
    s = lax.axis_index("sub")
    g = lax.axis_index("grp")
    _, tiles, bands, rows, _ = stiff_ref.shape
    vectors = defl_ref.shape[1]
    slots = off_ref.shape[0]
    overlap = place_ref.shape[3]
    rim = bands // 2
    halo = rim * rows
    width = tiles * rows
    columns = vectors * (slots + 1)
    share = out_ref.shape[1]
    count = len(OFFSETS)
    has_left = g > 0
    has_right = g < layers - 1

    barrier = pltpu.get_barrier_semaphore()
    for offset in SEND_ORDER:
        pl.semaphore_signal(
            barrier, inc=1, device_id=(lax.rem(s + offset + subs, subs), g), device_id_type=MESH
        )
    for step in range(1, layers):
        pl.semaphore_signal(
            barrier, inc=1, device_id=(s, lax.rem(g + step, layers)), device_id_type=MESH
        )

    inputs = [
        pltpu.make_async_copy(off_hbm, off_ref, in_sem.at[0]),
        pltpu.make_async_copy(need_hbm, need_ref, in_sem.at[1]),
        pltpu.make_async_copy(place_hbm, place_ref, in_sem.at[2]),
        pltpu.make_async_copy(
            defl_ref.at[0], basis.at[0, :, pl.ds(halo, width)], in_sem.at[3]
        ),
    ]
    for copy in inputs:
        copy.start()

    def stiff_copy(t):
        return pltpu.make_async_copy(stiff_ref.at[0, t], a_buf.at[t], a_sem.at[t])

    edges = list(range(rim)) + list(range(tiles - rim, tiles))

    for k in range(count):
        products[k * (overlap + 1) + overlap] = jnp.zeros((bands, vectors, rows), products.dtype)

    @pl.when(jnp.logical_not(has_left))
    def _():
        basis[0, :, 0:halo] = jnp.zeros((vectors, halo), basis.dtype)
        rim_in[:, 0] = jnp.zeros((count, vectors, halo), rim_in.dtype)

    @pl.when(jnp.logical_not(has_right))
    def _():
        basis[0, :, halo + width :] = jnp.zeros((vectors, halo), basis.dtype)
        rim_in[:, 1] = jnp.zeros((count, vectors, halo), rim_in.dtype)

    for copy in inputs:
        copy.wait()
    for t in range(tiles):
        stiff_copy(t).start()
    for u in range(tiles):
        own_tiles[u] = basis[0, :, halo + u * rows : halo + (u + 1) * rows]
    for k, offset in enumerate(OFFSETS):
        target = lax.rem(s + offset + subs, subs)
        for o in range(overlap):
            tile = jnp.int32(0)
            for n in range(slots):
                match = (off_ref[n, target] == -offset).astype(jnp.int32)
                tile = tile + match * need_ref[0, n, o, target]
            outgoing[k, o] = own_tiles[tile]

    def column(t):
        return t * rows if isinstance(t, int) else pl.multiple_of(t * rows, rows)

    def image_of(t):
        running = None
        for b in range(bands):
            term = dot_nt(basis[0, :, pl.ds(column(t + b), rows)], a_buf[t, b])
            running = term if running is None else running + term
        image[t] = running.astype(image.dtype)

    def left_of(c):
        running = None
        for b in range(bands):
            t = c - b
            if not 0 <= t < tiles:
                continue
            term = dot_nn(basis[0, :, (t + rim) * rows : (t + rim + 1) * rows], a_buf[t, b])
            running = term if running is None else running + term
        left_image[c, 0:vectors] = running.astype(left_image.dtype)

    group = bands - 1
    ahead = group
    waits_long = s < RCH - 1

    def own_tiles_from(start, stop):
        for first in range(start, stop, group):
            for t in range(first, min(first + group, stop)):
                stiff_copy(t).wait()
            for t in range(first, min(first + group, stop)):
                if rim <= t < tiles - rim:
                    image_of(t)
                left_of(t)

    @pl.when(waits_long)
    def _():
        own_tiles_from(0, ahead)

    pl.semaphore_wait(barrier, count + layers - 1)

    def sub_copy(k, offset):
        back = count - 1 - k
        return pltpu.make_async_remote_copy(
            src_ref=outgoing.at[k],
            dst_ref=arrived.at[pl.ds(back * (overlap + 1), overlap)],
            send_sem=sub_send.at[k],
            recv_sem=sub_recv.at[back],
            device_id=(lax.rem(s + offset + subs, subs), g),
            device_id_type=MESH,
        )

    lower = s < subs // 2
    for near, far in zip(NEAR_FIRST, SEND_ORDER):
        k, offset = OFFSETS.index(near), near
        if near != far:
            k = jnp.where(lower, k, OFFSETS.index(far))
            offset = jnp.where(lower, near, far)
        sub_copy(k, offset).start()

    def own_copy(to_left):
        source, target = (halo, halo + width) if to_left else (width, 0)
        return pltpu.make_async_remote_copy(
            src_ref=basis.at[0, :, pl.ds(source, halo)],
            dst_ref=basis.at[0, :, pl.ds(target, halo)],
            send_sem=own_send.at[0 if to_left else 1],
            recv_sem=own_recv.at[1 if to_left else 0],
            device_id=(s, g - 1 if to_left else g + 1),
            device_id_type=MESH,
        )

    def rim_copy(k):
        def make(to_left):
            source, target = (0, 1) if to_left else (1, 0)
            return pltpu.make_async_remote_copy(
                src_ref=rim_out.at[k, source],
                dst_ref=rim_in.at[k, target],
                send_sem=rim_send.at[k, 0 if to_left else 1],
                recv_sem=rim_recv.at[k, 1 if to_left else 0],
                device_id=(s, g - 1 if to_left else g + 1),
                device_id_type=MESH,
            )

        return make

    def start_pair(make):
        @pl.when(has_left)
        def _():
            make(True).start()

        @pl.when(has_right)
        def _():
            make(False).start()

    def wait_pair(make):
        @pl.when(has_left)
        def _():
            make(False).wait_recv()
            make(True).wait_send()

        @pl.when(has_right)
        def _():
            make(True).wait_recv()
            make(False).wait_send()

    start_pair(own_copy)

    def first_of(n):
        offset = off_ref[n, s]
        return (offset + RCH - (offset > 0).astype(jnp.int32)) * (overlap + 1)

    blank = overlap
    hits = [
        [[(place_ref[0, n, 0, o] == u).astype(jnp.int32) for o in range(overlap)] for n in range(slots)]
        for u in range(tiles)
    ]
    shift = [
        [sum((o - blank) * hits[u][n][o] for o in range(overlap)) for n in range(slots)]
        for u in range(tiles)
    ]
    for n in range(slots):
        for u in range(tiles):
            found_at[n * tiles + u] = first_of(n) + blank + shift[u][n]
    for k, offset in enumerate(OFFSETS):
        for i, u in enumerate(edges):
            spot = k * (overlap + 1) + blank
            for n in range(slots):
                spot = spot + (off_ref[n, s] == offset).astype(jnp.int32) * shift[u][n]
            rim_found_at[k * len(edges) + i] = spot
        for o in range(overlap):
            spot = jnp.int32(0)
            for n in range(slots):
                spot = spot + (off_ref[n, s] == offset).astype(jnp.int32) * place_ref[0, n, 0, o]
            spot_at[k * overlap + o] = spot

    @pl.when(jnp.logical_not(waits_long))
    def _():
        own_tiles_from(0, ahead)

    own_tiles_from(ahead, tiles)
    for c in range(tiles, tiles + 2 * rim):
        left_of(c)
    wait_pair(own_copy)
    for t in edges:
        image_of(t)
    corner = None
    for t in range(tiles):
        term = dot_nt(basis[0, :, halo + t * rows : halo + (t + 1) * rows], image[t])
        corner = term if corner is None else corner + term
    part[0:vectors, 0:vectors] = corner

    def land(k):
        sent = count - 1 - k
        if isinstance(k, int):
            offset = OFFSETS[sent]
        else:
            offset = sent - RCH + (sent >= RCH).astype(jnp.int32)
        sub_copy(sent, offset).wait_recv()
        for i in range(len(edges)):
            tile = jnp.zeros((vectors, rows), arrived.dtype)
            for o in range(overlap):
                hit = rim_found_at[k * len(edges) + i] == k * (overlap + 1) + o
                tile = jnp.where(hit, arrived[k * (overlap + 1) + o], tile)
            lane = i % rim * rows
            rim_out[k, i // rim, :, lane : lane + rows] = tile
        for o in range(overlap):
            spot = spot_at[k * overlap + o]
            for b in range(bands):
                term = dot_nn(arrived[k * (overlap + 1) + o], a_buf[spot, b])
                products[k * (overlap + 1) + o, b] = term.astype(products.dtype)
            if o == 0:
                start_pair(rim_copy(k))

    beside_end = jnp.logical_or(s == RCH - 1, s == subs - 1)
    land(jnp.where(waits_long, 3, 1))
    land(jnp.where(waits_long, 2, 0))
    land(jnp.where(waits_long, 1, jnp.where(beside_end, 3, 2)))
    land(jnp.where(waits_long, 0, jnp.where(beside_end, 2, 3)))
    for c in range(tiles + 2 * rim):
        for n in range(slots):
            total = None
            for b in range(bands):
                t = c - b
                if 0 <= t < tiles:
                    term = products[found_at[n * tiles + t], b]
                    total = term if total is None else total + term
            left_image[c, (n + 1) * vectors : (n + 2) * vectors] = total
    for k in range(count):
        sub_copy(k, OFFSETS[k]).wait_send()

    for n in range(slots):
        low = below = None
        for o in range(overlap):
            tile = arrived[first_of(n) + o]
            spot = place_ref[0, n, 0, o]
            term = dot_nt(tile, image[spot])
            low = term if low is None else low + term
            term = dot_nt(left_image[rim + spot], tile)
            below = term if below is None else below + term
        lines = slice((n + 1) * vectors, (n + 2) * vectors)
        part[lines, 0:vectors] = low
        part[:, lines] = below

    def edge_partial(i):
        lane = i % rim * rows
        right = jnp.concatenate(
            [
                rim_in[off_ref[n, s] + RCH - (off_ref[n, s] > 0).astype(jnp.int32), i // rim, :, lane : lane + rows]
                for n in range(slots)
            ]
        )
        return dot_nt(left_image[i if i < rim else tiles + i], right)

    for k in range(count):
        wait_pair(rim_copy(k))
    sides = None
    for i in range(2 * rim):
        term = edge_partial(i)
        sides = term if sides is None else sides + term
    part[:, vectors:] += sides
    part_low[...] = part[...].astype(part_low.dtype)

    red_copies = []
    for step in range(1, layers):
        peer = lax.rem(g + step, layers)
        red_copies.append(
            pltpu.make_async_remote_copy(
                src_ref=part_low.at[pl.ds(pl.multiple_of(peer * share, share), share)],
                dst_ref=shares.at[step - 1],
                send_sem=red_send.at[step - 1],
                recv_sem=red_recv.at[step - 1],
                device_id=(s, peer),
                device_id_type=MESH,
            )
        )
    for copy in red_copies:
        copy.start()
    for copy in red_copies:
        copy.wait()
    result = part[pl.ds(pl.multiple_of(g * share, share), share), :]
    for step in range(1, layers):
        result = result + shares[step - 1].astype(jnp.float32)
    out_ref[0] = result


def on_device(subs, layers, stiffness, deflation, off_map, need_map, place_map):
    _, tiles, bands, rows, _ = stiffness.shape
    _, vectors, width = deflation.shape
    slots, overlap = place_map.shape[2:]
    columns = vectors * (slots + 1)
    halo = (bands // 2) * rows
    share = columns // layers
    count = len(OFFSETS)
    low = deflation.dtype
    dma = pltpu.SemaphoreType.DMA
    tables = (
        off_map.T,
        need_map.transpose(1, 2, 3, 0),
        place_map.transpose(0, 2, 1, 3),
    )
    return pl.pallas_call(
        functools.partial(kernel, subs, layers),
        out_shape=pltpu.VMEM((1, share, columns), jnp.float32),
        in_specs=[pl.BlockSpec(memory_space=pl.ANY)] * 5,
        out_specs=pl.BlockSpec(memory_space=pltpu.VMEM),
        scratch_shapes=[
            *[pltpu.SMEM(table.shape, table.dtype) for table in tables],
            pltpu.VMEM((tiles, bands, rows, rows), low),
            pltpu.VMEM((1, vectors, width + 2 * halo), low),
            pltpu.VMEM((tiles, vectors, rows), low),
            pltpu.VMEM((tiles + 2 * (bands // 2), columns, rows), low),
            pltpu.VMEM((tiles, vectors, rows), low),
            pltpu.VMEM((count, overlap, vectors, rows), low),
            pltpu.VMEM((count * (overlap + 1), vectors, rows), low),
            pltpu.VMEM((count * (overlap + 1), bands, vectors, rows), low),
            pltpu.VMEM((count, 2, vectors, halo), low),
            pltpu.VMEM((count, 2, vectors, halo), low),
            pltpu.SMEM((slots * tiles,), jnp.int32),
            pltpu.SMEM((count * 2 * (bands // 2),), jnp.int32),
            pltpu.SMEM((count * overlap,), jnp.int32),
            pltpu.VMEM((columns, columns), jnp.float32),
            pltpu.VMEM((columns, columns), low),
            pltpu.VMEM((layers - 1, share, columns), low),
            dma((4,)),
            dma((tiles,)),
            dma((count,)), dma((count,)),
            dma((2,)), dma((2,)),
            dma((count, 2)), dma((count, 2)),
            dma((layers - 1,)), dma((layers - 1,)),
        ],
        compiler_params=pltpu.CompilerParams(collective_id=0, has_side_effects=True),
    )(*tables, deflation, stiffness)


def solution(mesh):
    in_specs = (
        P("sub", "grp", None, None, None),
        P("sub", None, "grp"),
        P(),
        P(None, "grp", None, None),
        P("sub", "grp", None, None),
    )
    out_specs = P("sub", "grp", None)
    return jax.shard_map(
        functools.partial(on_device, mesh.shape["sub"], mesh.shape["grp"]),
        mesh=mesh,
        in_specs=in_specs,
        out_specs=out_specs,
        check_vma=False,
    )
```

```python
import functools

import jax
import jax.numpy as jnp
from jax import lax
from jax.experimental import pallas as pl
from jax.experimental.pallas import tpu as pltpu
from jax.sharding import PartitionSpec as P

RCH = 2
MESH = pl.DeviceIdType.MESH
OFFSETS = [value for value in range(-RCH, RCH + 1) if value != 0]
SEND_ORDER = sorted(OFFSETS, key=lambda value: (value < 0, abs(value)))
NEAR_FIRST = [1, 2, -2, -1]
NT = (((1,), (1,)), ((), ()))
NN = (((1,), (0,)), ((), ()))


def dot_nt(lhs, rhs):
    return lax.dot_general(lhs, rhs, NT, preferred_element_type=jnp.float32)


def dot_nn(lhs, rhs):
    return lax.dot_general(lhs, rhs, NN, preferred_element_type=jnp.float32)


def kernel(
    subs, layers, off_hbm, need_hbm, place_hbm, defl_ref, stiff_ref, out_ref,
    off_ref, need_ref, place_ref, a_buf, basis, image, left_image, own_tiles, outgoing, arrived,
    products, rim_out, rim_in, found_at, rim_found_at, spot_at, part, part_low, shares,
    in_sem, a_sem, sub_send, sub_recv, own_send, own_recv, rim_send, rim_recv, red_send, red_recv,
):
    s = lax.axis_index("sub")
    g = lax.axis_index("grp")
    _, tiles, bands, rows, _ = stiff_ref.shape
    vectors = defl_ref.shape[1]
    slots = off_ref.shape[0]
    overlap = place_ref.shape[3]
    rim = bands // 2
    halo = rim * rows
    width = tiles * rows
    columns = vectors * (slots + 1)
    share = out_ref.shape[1]
    count = len(OFFSETS)
    has_left = g > 0
    has_right = g < layers - 1

    barrier = pltpu.get_barrier_semaphore()
    for offset in SEND_ORDER:
        pl.semaphore_signal(
            barrier, inc=1, device_id=(lax.rem(s + offset + subs, subs), g), device_id_type=MESH
        )
    for step in range(1, layers):
        pl.semaphore_signal(
            barrier, inc=1, device_id=(s, lax.rem(g + step, layers)), device_id_type=MESH
        )

    inputs = [
        pltpu.make_async_copy(off_hbm, off_ref, in_sem.at[0]),
        pltpu.make_async_copy(need_hbm, need_ref, in_sem.at[1]),
        pltpu.make_async_copy(place_hbm, place_ref, in_sem.at[2]),
        pltpu.make_async_copy(
            defl_ref.at[0], basis.at[0, :, pl.ds(halo, width)], in_sem.at[3]
        ),
    ]
    for copy in inputs:
        copy.start()

    def stiff_copy(t):
        return pltpu.make_async_copy(stiff_ref.at[0, t], a_buf.at[t], a_sem.at[t])

    edges = list(range(rim)) + list(range(tiles - rim, tiles))

    for k in range(count):
        products[k * (overlap + 1) + overlap] = jnp.zeros((bands, vectors, rows), products.dtype)

    @pl.when(jnp.logical_not(has_left))
    def _():
        basis[0, :, 0:halo] = jnp.zeros((vectors, halo), basis.dtype)
        rim_in[:, 0] = jnp.zeros((count, vectors, halo), rim_in.dtype)

    @pl.when(jnp.logical_not(has_right))
    def _():
        basis[0, :, halo + width :] = jnp.zeros((vectors, halo), basis.dtype)
        rim_in[:, 1] = jnp.zeros((count, vectors, halo), rim_in.dtype)

    for copy in inputs:
        copy.wait()
    for t in range(tiles):
        stiff_copy(t).start()
    for u in range(tiles):
        own_tiles[u] = basis[0, :, halo + u * rows : halo + (u + 1) * rows]
    for k, offset in enumerate(OFFSETS):
        target = lax.rem(s + offset + subs, subs)
        for o in range(overlap):
            tile = jnp.int32(0)
            for n in range(slots):
                match = (off_ref[n, target] == -offset).astype(jnp.int32)
                tile = tile + match * need_ref[0, n, o, target]
            outgoing[k, o] = own_tiles[tile]

    def column(t):
        return t * rows if isinstance(t, int) else pl.multiple_of(t * rows, rows)

    def image_of(t):
        running = None
        for b in range(bands):
            term = dot_nt(basis[0, :, pl.ds(column(t + b), rows)], a_buf[t, b])
            running = term if running is None else running + term
        image[t] = running.astype(image.dtype)

    def left_of(c):
        running = None
        for b in range(bands):
            t = c - b
            if not 0 <= t < tiles:
                continue
            term = dot_nn(basis[0, :, (t + rim) * rows : (t + rim + 1) * rows], a_buf[t, b])
            running = term if running is None else running + term
        left_image[c, 0:vectors] = running.astype(left_image.dtype)

    group = bands - 1
    ahead = group
    waits_long = s < RCH - 1

    def own_tiles_from(start, stop):
        for first in range(start, stop, group):
            for t in range(first, min(first + group, stop)):
                stiff_copy(t).wait()
            for t in range(first, min(first + group, stop)):
                if rim <= t < tiles - rim:
                    image_of(t)
                left_of(t)

    @pl.when(waits_long)
    def _():
        own_tiles_from(0, ahead)

    pl.semaphore_wait(barrier, count + layers - 1)

    def sub_copy(k, offset):
        back = count - 1 - k
        return pltpu.make_async_remote_copy(
            src_ref=outgoing.at[k],
            dst_ref=arrived.at[pl.ds(back * (overlap + 1), overlap)],
            send_sem=sub_send.at[k],
            recv_sem=sub_recv.at[back],
            device_id=(lax.rem(s + offset + subs, subs), g),
            device_id_type=MESH,
        )

    lower = s < subs // 2
    for near, far in zip(NEAR_FIRST, SEND_ORDER):
        k, offset = OFFSETS.index(near), near
        if near != far:
            k = jnp.where(lower, k, OFFSETS.index(far))
            offset = jnp.where(lower, near, far)
        sub_copy(k, offset).start()

    def own_copy(to_left):
        source, target = (halo, halo + width) if to_left else (width, 0)
        return pltpu.make_async_remote_copy(
            src_ref=basis.at[0, :, pl.ds(source, halo)],
            dst_ref=basis.at[0, :, pl.ds(target, halo)],
            send_sem=own_send.at[0 if to_left else 1],
            recv_sem=own_recv.at[1 if to_left else 0],
            device_id=(s, g - 1 if to_left else g + 1),
            device_id_type=MESH,
        )

    def rim_copy(k):
        def make(to_left):
            source, target = (0, 1) if to_left else (1, 0)
            return pltpu.make_async_remote_copy(
                src_ref=rim_out.at[k, source],
                dst_ref=rim_in.at[k, target],
                send_sem=rim_send.at[k, 0 if to_left else 1],
                recv_sem=rim_recv.at[k, 1 if to_left else 0],
                device_id=(s, g - 1 if to_left else g + 1),
                device_id_type=MESH,
            )

        return make

    def start_pair(make):
        @pl.when(has_left)
        def _():
            make(True).start()

        @pl.when(has_right)
        def _():
            make(False).start()

    def wait_pair(make):
        @pl.when(has_left)
        def _():
            make(False).wait_recv()
            make(True).wait_send()

        @pl.when(has_right)
        def _():
            make(True).wait_recv()
            make(False).wait_send()

    start_pair(own_copy)

    def first_of(n):
        offset = off_ref[n, s]
        return (offset + RCH - (offset > 0).astype(jnp.int32)) * (overlap + 1)

    blank = overlap
    hits = [
        [[(place_ref[0, n, 0, o] == u).astype(jnp.int32) for o in range(overlap)] for n in range(slots)]
        for u in range(tiles)
    ]
    shift = [
        [sum((o - blank) * hits[u][n][o] for o in range(overlap)) for n in range(slots)]
        for u in range(tiles)
    ]
    for n in range(slots):
        for u in range(tiles):
            found_at[n * tiles + u] = first_of(n) + blank + shift[u][n]
    for k, offset in enumerate(OFFSETS):
        for i, u in enumerate(edges):
            spot = k * (overlap + 1) + blank
            for n in range(slots):
                spot = spot + (off_ref[n, s] == offset).astype(jnp.int32) * shift[u][n]
            rim_found_at[k * len(edges) + i] = spot
        for o in range(overlap):
            spot = jnp.int32(0)
            for n in range(slots):
                spot = spot + (off_ref[n, s] == offset).astype(jnp.int32) * place_ref[0, n, 0, o]
            spot_at[k * overlap + o] = spot

    @pl.when(jnp.logical_not(waits_long))
    def _():
        own_tiles_from(0, ahead)

    own_tiles_from(ahead, tiles)
    for c in range(tiles, tiles + 2 * rim):
        left_of(c)
    wait_pair(own_copy)
    for t in edges:
        image_of(t)
    corner = None
    for t in range(tiles):
        term = dot_nt(basis[0, :, halo + t * rows : halo + (t + 1) * rows], image[t])
        corner = term if corner is None else corner + term
    part[0:vectors, 0:vectors] = corner

    def land(k):
        sent = count - 1 - k
        if isinstance(k, int):
            offset = OFFSETS[sent]
        else:
            offset = sent - RCH + (sent >= RCH).astype(jnp.int32)
        sub_copy(sent, offset).wait_recv()
        for i in range(len(edges)):
            tile = jnp.zeros((vectors, rows), arrived.dtype)
            for o in range(overlap):
                hit = rim_found_at[k * len(edges) + i] == k * (overlap + 1) + o
                tile = jnp.where(hit, arrived[k * (overlap + 1) + o], tile)
            lane = i % rim * rows
            rim_out[k, i // rim, :, lane : lane + rows] = tile

    def multiply(k, some):
        for o in some:
            spot = spot_at[k * overlap + o]
            for b in range(bands):
                term = dot_nn(arrived[k * (overlap + 1) + o], a_buf[spot, b])
                products[k * (overlap + 1) + o, b] = term.astype(products.dtype)

    def finish(k):
        multiply(k, range(1))
        start_pair(rim_copy(k))
        multiply(k, range(1, overlap))

    beside_end = jnp.logical_or(s == RCH - 1, s == subs - 1)
    together = s < RCH
    for k in (jnp.where(waits_long, 3, 1), jnp.where(waits_long, 2, 0)):
        land(k)
        finish(k)
    third = jnp.where(waits_long, 1, jnp.where(beside_end, 3, 2))
    last = jnp.where(waits_long, 0, jnp.where(beside_end, 2, 3))
    land(third)

    @pl.when(jnp.logical_not(together))
    def _():
        finish(third)

    land(last)

    @pl.when(together)
    def _():
        multiply(third, range(1))
        start_pair(rim_copy(third))

    finish(last)

    @pl.when(together)
    def _():
        multiply(third, range(1, overlap))

    for c in range(tiles + 2 * rim):
        for n in range(slots):
            total = None
            for b in range(bands):
                t = c - b
                if 0 <= t < tiles:
                    term = products[found_at[n * tiles + t], b]
                    total = term if total is None else total + term
            left_image[c, (n + 1) * vectors : (n + 2) * vectors] = total
    for k in range(count):
        sub_copy(k, OFFSETS[k]).wait_send()

    for n in range(slots):
        low = below = None
        for o in range(overlap):
            tile = arrived[first_of(n) + o]
            spot = place_ref[0, n, 0, o]
            term = dot_nt(tile, image[spot])
            low = term if low is None else low + term
            term = dot_nt(left_image[rim + spot], tile)
            below = term if below is None else below + term
        lines = slice((n + 1) * vectors, (n + 2) * vectors)
        part[lines, 0:vectors] = low
        part[:, lines] = below

    def edge_partial(i):
        lane = i % rim * rows
        right = jnp.concatenate(
            [
                rim_in[off_ref[n, s] + RCH - (off_ref[n, s] > 0).astype(jnp.int32), i // rim, :, lane : lane + rows]
                for n in range(slots)
            ]
        )
        return dot_nt(left_image[i if i < rim else tiles + i], right)

    for k in range(count):
        wait_pair(rim_copy(k))
    sides = None
    for i in range(2 * rim):
        term = edge_partial(i)
        sides = term if sides is None else sides + term
    part[:, vectors:] += sides
    part_low[...] = part[...].astype(part_low.dtype)

    red_copies = []
    for step in range(1, layers):
        peer = lax.rem(g + step, layers)
        red_copies.append(
            pltpu.make_async_remote_copy(
                src_ref=part_low.at[pl.ds(pl.multiple_of(peer * share, share), share)],
                dst_ref=shares.at[step - 1],
                send_sem=red_send.at[step - 1],
                recv_sem=red_recv.at[step - 1],
                device_id=(s, peer),
                device_id_type=MESH,
            )
        )
    for copy in red_copies:
        copy.start()
    for copy in red_copies:
        copy.wait()
    result = part[pl.ds(pl.multiple_of(g * share, share), share), :]
    for step in range(1, layers):
        result = result + shares[step - 1].astype(jnp.float32)
    out_ref[0] = result


def on_device(subs, layers, stiffness, deflation, off_map, need_map, place_map):
    _, tiles, bands, rows, _ = stiffness.shape
    _, vectors, width = deflation.shape
    slots, overlap = place_map.shape[2:]
    columns = vectors * (slots + 1)
    halo = (bands // 2) * rows
    share = columns // layers
    count = len(OFFSETS)
    low = deflation.dtype
    dma = pltpu.SemaphoreType.DMA
    tables = (
        off_map.T,
        need_map.transpose(1, 2, 3, 0),
        place_map.transpose(0, 2, 1, 3),
    )
    return pl.pallas_call(
        functools.partial(kernel, subs, layers),
        out_shape=pltpu.VMEM((1, share, columns), jnp.float32),
        in_specs=[pl.BlockSpec(memory_space=pl.ANY)] * 5,
        out_specs=pl.BlockSpec(memory_space=pltpu.VMEM),
        scratch_shapes=[
            *[pltpu.SMEM(table.shape, table.dtype) for table in tables],
            pltpu.VMEM((tiles, bands, rows, rows), low),
            pltpu.VMEM((1, vectors, width + 2 * halo), low),
            pltpu.VMEM((tiles, vectors, rows), low),
            pltpu.VMEM((tiles + 2 * (bands // 2), columns, rows), low),
            pltpu.VMEM((tiles, vectors, rows), low),
            pltpu.VMEM((count, overlap, vectors, rows), low),
            pltpu.VMEM((count * (overlap + 1), vectors, rows), low),
            pltpu.VMEM((count * (overlap + 1), bands, vectors, rows), low),
            pltpu.VMEM((count, 2, vectors, halo), low),
            pltpu.VMEM((count, 2, vectors, halo), low),
            pltpu.SMEM((slots * tiles,), jnp.int32),
            pltpu.SMEM((count * 2 * (bands // 2),), jnp.int32),
            pltpu.SMEM((count * overlap,), jnp.int32),
            pltpu.VMEM((columns, columns), jnp.float32),
            pltpu.VMEM((columns, columns), low),
            pltpu.VMEM((layers - 1, share, columns), low),
            dma((4,)),
            dma((tiles,)),
            dma((count,)), dma((count,)),
            dma((2,)), dma((2,)),
            dma((count, 2)), dma((count, 2)),
            dma((layers - 1,)), dma((layers - 1,)),
        ],
        compiler_params=pltpu.CompilerParams(collective_id=0, has_side_effects=True),
    )(*tables, deflation, stiffness)


def solution(mesh):
    in_specs = (
        P("sub", "grp", None, None, None),
        P("sub", None, "grp"),
        P(),
        P(None, "grp", None, None),
        P("sub", "grp", None, None),
    )
    out_specs = P("sub", "grp", None)
    return jax.shard_map(
        functools.partial(on_device, mesh.shape["sub"], mesh.shape["grp"]),
        mesh=mesh,
        in_specs=in_specs,
        out_specs=out_specs,
        check_vma=False,
    )
```

```python
import functools

import jax
import jax.numpy as jnp
from jax import lax
from jax.experimental import pallas as pl
from jax.experimental.pallas import tpu as pltpu
from jax.sharding import PartitionSpec as P

RCH = 2
MESH = pl.DeviceIdType.MESH
OFFSETS = [value for value in range(-RCH, RCH + 1) if value != 0]
SEND_ORDER = sorted(OFFSETS, key=lambda value: (value < 0, abs(value)))
NEAR_FIRST = [1, 2, -2, -1]
NT = (((1,), (1,)), ((), ()))
NN = (((1,), (0,)), ((), ()))


def dot_nt(lhs, rhs):
    return lax.dot_general(lhs, rhs, NT, preferred_element_type=jnp.float32)


def dot_nn(lhs, rhs):
    return lax.dot_general(lhs, rhs, NN, preferred_element_type=jnp.float32)


def kernel(
    subs, layers, off_hbm, need_hbm, place_hbm, defl_ref, stiff_ref, out_ref,
    off_ref, need_ref, place_ref, a_buf, basis, image, left_image, own_tiles, outgoing, arrived,
    products, rim_out, rim_in, found_at, rim_found_at, spot_at, part, part_low, shares,
    in_sem, a_sem, sub_send, sub_recv, own_send, own_recv, rim_send, rim_recv, red_send, red_recv,
):
    s = lax.axis_index("sub")
    g = lax.axis_index("grp")
    _, tiles, bands, rows, _ = stiff_ref.shape
    vectors = defl_ref.shape[1]
    slots = off_ref.shape[0]
    overlap = place_ref.shape[3]
    rim = bands // 2
    halo = rim * rows
    width = tiles * rows
    columns = vectors * (slots + 1)
    share = out_ref.shape[1]
    count = len(OFFSETS)
    has_left = g > 0
    has_right = g < layers - 1

    barrier = pltpu.get_barrier_semaphore()
    for offset in SEND_ORDER:
        pl.semaphore_signal(
            barrier, inc=1, device_id=(lax.rem(s + offset + subs, subs), g), device_id_type=MESH
        )
    for step in range(1, layers):
        pl.semaphore_signal(
            barrier, inc=1, device_id=(s, lax.rem(g + step, layers)), device_id_type=MESH
        )

    inputs = [
        pltpu.make_async_copy(off_hbm, off_ref, in_sem.at[0]),
        pltpu.make_async_copy(need_hbm, need_ref, in_sem.at[1]),
        pltpu.make_async_copy(place_hbm, place_ref, in_sem.at[2]),
        pltpu.make_async_copy(
            defl_ref.at[0], basis.at[0, :, pl.ds(halo, width)], in_sem.at[3]
        ),
    ]
    for copy in inputs:
        copy.start()

    def stiff_copy(t):
        return pltpu.make_async_copy(stiff_ref.at[0, t], a_buf.at[t], a_sem.at[t])

    edges = list(range(rim)) + list(range(tiles - rim, tiles))

    for k in range(count):
        products[k * (overlap + 1) + overlap] = jnp.zeros((bands, vectors, rows), products.dtype)

    @pl.when(jnp.logical_not(has_left))
    def _():
        basis[0, :, 0:halo] = jnp.zeros((vectors, halo), basis.dtype)
        rim_in[:, 0] = jnp.zeros((count, vectors, halo), rim_in.dtype)

    @pl.when(jnp.logical_not(has_right))
    def _():
        basis[0, :, halo + width :] = jnp.zeros((vectors, halo), basis.dtype)
        rim_in[:, 1] = jnp.zeros((count, vectors, halo), rim_in.dtype)

    for copy in inputs:
        copy.wait()
    for t in range(tiles):
        stiff_copy(t).start()
    for u in range(tiles):
        own_tiles[u] = basis[0, :, halo + u * rows : halo + (u + 1) * rows]
    for k, offset in enumerate(OFFSETS):
        target = lax.rem(s + offset + subs, subs)
        for o in range(overlap):
            tile = jnp.int32(0)
            for n in range(slots):
                match = (off_ref[n, target] == -offset).astype(jnp.int32)
                tile = tile + match * need_ref[0, n, o, target]
            outgoing[k, o] = own_tiles[tile]

    def column(t):
        return t * rows if isinstance(t, int) else pl.multiple_of(t * rows, rows)

    def image_of(t):
        running = None
        for b in range(bands):
            term = dot_nt(basis[0, :, pl.ds(column(t + b), rows)], a_buf[t, b])
            running = term if running is None else running + term
        image[t] = running.astype(image.dtype)

    def left_of(c):
        running = None
        for b in range(bands):
            t = c - b
            if not 0 <= t < tiles:
                continue
            term = dot_nn(basis[0, :, (t + rim) * rows : (t + rim + 1) * rows], a_buf[t, b])
            running = term if running is None else running + term
        left_image[c, 0:vectors] = running.astype(left_image.dtype)

    group = bands - 1
    ahead = group
    waits_long = s < RCH - 1

    def own_tiles_from(start, stop):
        for first in range(start, stop, group):
            for t in range(first, min(first + group, stop)):
                stiff_copy(t).wait()
            for t in range(first, min(first + group, stop)):
                if rim <= t < tiles - rim:
                    image_of(t)
                left_of(t)

    @pl.when(waits_long)
    def _():
        own_tiles_from(0, ahead)

    pl.semaphore_wait(barrier, count + layers - 1)

    def sub_copy(k, offset):
        back = count - 1 - k
        return pltpu.make_async_remote_copy(
            src_ref=outgoing.at[k],
            dst_ref=arrived.at[pl.ds(back * (overlap + 1), overlap)],
            send_sem=sub_send.at[k],
            recv_sem=sub_recv.at[back],
            device_id=(lax.rem(s + offset + subs, subs), g),
            device_id_type=MESH,
        )

    lower = s < subs // 2
    for near, far in zip(NEAR_FIRST, SEND_ORDER):
        k, offset = OFFSETS.index(near), near
        if near != far:
            k = jnp.where(lower, k, OFFSETS.index(far))
            offset = jnp.where(lower, near, far)
        sub_copy(k, offset).start()

    def own_copy(to_left):
        source, target = (halo, halo + width) if to_left else (width, 0)
        return pltpu.make_async_remote_copy(
            src_ref=basis.at[0, :, pl.ds(source, halo)],
            dst_ref=basis.at[0, :, pl.ds(target, halo)],
            send_sem=own_send.at[0 if to_left else 1],
            recv_sem=own_recv.at[1 if to_left else 0],
            device_id=(s, g - 1 if to_left else g + 1),
            device_id_type=MESH,
        )

    def rim_copy(k):
        def make(to_left):
            source, target = (0, 1) if to_left else (1, 0)
            return pltpu.make_async_remote_copy(
                src_ref=rim_out.at[k, source],
                dst_ref=rim_in.at[k, target],
                send_sem=rim_send.at[k, 0 if to_left else 1],
                recv_sem=rim_recv.at[k, 1 if to_left else 0],
                device_id=(s, g - 1 if to_left else g + 1),
                device_id_type=MESH,
            )

        return make

    def start_pair(make):
        @pl.when(has_left)
        def _():
            make(True).start()

        @pl.when(has_right)
        def _():
            make(False).start()

    def wait_pair(make):
        @pl.when(has_left)
        def _():
            make(False).wait_recv()
            make(True).wait_send()

        @pl.when(has_right)
        def _():
            make(True).wait_recv()
            make(False).wait_send()

    start_pair(own_copy)

    def first_of(n):
        offset = off_ref[n, s]
        return (offset + RCH - (offset > 0).astype(jnp.int32)) * (overlap + 1)

    blank = overlap
    hits = [
        [[(place_ref[0, n, 0, o] == u).astype(jnp.int32) for o in range(overlap)] for n in range(slots)]
        for u in range(tiles)
    ]
    shift = [
        [sum((o - blank) * hits[u][n][o] for o in range(overlap)) for n in range(slots)]
        for u in range(tiles)
    ]
    for n in range(slots):
        for u in range(tiles):
            found_at[n * tiles + u] = first_of(n) + blank + shift[u][n]
    for k, offset in enumerate(OFFSETS):
        for i, u in enumerate(edges):
            spot = k * (overlap + 1) + blank
            for n in range(slots):
                spot = spot + (off_ref[n, s] == offset).astype(jnp.int32) * shift[u][n]
            rim_found_at[k * len(edges) + i] = spot
        for o in range(overlap):
            spot = jnp.int32(0)
            for n in range(slots):
                spot = spot + (off_ref[n, s] == offset).astype(jnp.int32) * place_ref[0, n, 0, o]
            spot_at[k * overlap + o] = spot

    @pl.when(jnp.logical_not(waits_long))
    def _():
        own_tiles_from(0, ahead)

    own_tiles_from(ahead, tiles)
    for c in range(tiles, tiles + 2 * rim):
        left_of(c)
    wait_pair(own_copy)
    for t in edges:
        image_of(t)
    corner = None
    for t in range(tiles):
        term = dot_nt(basis[0, :, halo + t * rows : halo + (t + 1) * rows], image[t])
        corner = term if corner is None else corner + term
    part[0:vectors, 0:vectors] = corner

    def land(k):
        sent = count - 1 - k
        if isinstance(k, int):
            offset = OFFSETS[sent]
        else:
            offset = sent - RCH + (sent >= RCH).astype(jnp.int32)
        sub_copy(sent, offset).wait_recv()
        for i in range(len(edges)):
            tile = jnp.zeros((vectors, rows), arrived.dtype)
            for o in range(overlap):
                hit = rim_found_at[k * len(edges) + i] == k * (overlap + 1) + o
                tile = jnp.where(hit, arrived[k * (overlap + 1) + o], tile)
            lane = i % rim * rows
            rim_out[k, i // rim, :, lane : lane + rows] = tile

    def multiply(k, some):
        for o in some:
            spot = spot_at[k * overlap + o]
            for b in range(bands):
                term = dot_nn(arrived[k * (overlap + 1) + o], a_buf[spot, b])
                products[k * (overlap + 1) + o, b] = term.astype(products.dtype)

    def finish(k):
        multiply(k, range(1))
        start_pair(rim_copy(k))
        multiply(k, range(1, overlap))

    beside_end = jnp.logical_or(s == RCH - 1, s == subs - 1)
    together = s < RCH
    for k in (jnp.where(waits_long, 3, 1), jnp.where(waits_long, 2, 0)):
        land(k)
        finish(k)
    third = jnp.where(waits_long, 1, jnp.where(beside_end, 3, 2))
    last = jnp.where(waits_long, 0, jnp.where(beside_end, 2, 3))
    land(third)

    @pl.when(jnp.logical_not(together))
    def _():
        finish(third)

    land(last)

    @pl.when(together)
    def _():
        multiply(third, range(1))
        start_pair(rim_copy(third))

    finish(last)

    @pl.when(together)
    def _():
        multiply(third, range(1, overlap))

    for c in range(tiles + 2 * rim):
        for n in range(slots):
            total = None
            for b in range(bands):
                t = c - b
                if 0 <= t < tiles:
                    term = products[found_at[n * tiles + t], b]
                    total = term if total is None else total + term
            left_image[c, (n + 1) * vectors : (n + 2) * vectors] = total
    for k in range(count):
        sub_copy(k, OFFSETS[k]).wait_send()

    for n in range(slots):
        low = below = None
        for o in range(overlap):
            tile = arrived[first_of(n) + o]
            spot = place_ref[0, n, 0, o]
            term = dot_nt(tile, image[spot])
            low = term if low is None else low + term
            term = dot_nt(left_image[rim + spot], tile)
            below = term if below is None else below + term
        lines = slice((n + 1) * vectors, (n + 2) * vectors)
        part[lines, 0:vectors] = low
        part[:, lines] = below

    def edge_basis(i):
        lane = i % rim * rows
        right = jnp.concatenate(
            [
                rim_in[off_ref[n, s] + RCH - (off_ref[n, s] > 0).astype(jnp.int32), i // rim, :, lane : lane + rows]
                for n in range(slots)
            ]
        )
        return right

    for k in range(count):
        wait_pair(rim_copy(k))
    rights = [edge_basis(i) for i in range(2 * rim)]
    cores = 2 if layers % 2 == 0 else 1
    chips = layers // cores
    red_copies = []
    for away in list(range(1, chips)) + [0]:
        chip = lax.rem(g // cores + away, chips)
        lines = pl.ds(pl.multiple_of(chip * cores * share, cores * share), cores * share)
        sides = None
        for i in range(2 * rim):
            term = dot_nt(left_image[i if i < rim else tiles + i, lines], rights[i])
            sides = term if sides is None else sides + term
        part[lines, vectors:] += sides
        part_low[lines] = part[lines].astype(part_low.dtype)
        for turn in range(cores if away else cores - 1):
            core = turn if away else lax.rem(g + 1 + turn, cores)
            peer = chip * cores + core
            step = lax.rem(peer - g + layers, layers)
            copy = pltpu.make_async_remote_copy(
                src_ref=part_low.at[pl.ds(pl.multiple_of(peer * share, share), share)],
                dst_ref=shares.at[step - 1],
                send_sem=red_send.at[step - 1],
                recv_sem=red_recv.at[step - 1],
                device_id=(s, peer),
                device_id_type=MESH,
            )
            copy.start()
            red_copies.append(copy)
    for copy in red_copies:
        copy.wait()
    result = part[pl.ds(pl.multiple_of(g * share, share), share), :]
    for step in range(1, layers):
        result = result + shares[step - 1].astype(jnp.float32)
    out_ref[0] = result


def on_device(subs, layers, stiffness, deflation, off_map, need_map, place_map):
    _, tiles, bands, rows, _ = stiffness.shape
    _, vectors, width = deflation.shape
    slots, overlap = place_map.shape[2:]
    columns = vectors * (slots + 1)
    halo = (bands // 2) * rows
    share = columns // layers
    count = len(OFFSETS)
    low = deflation.dtype
    dma = pltpu.SemaphoreType.DMA
    tables = (
        off_map.T,
        need_map.transpose(1, 2, 3, 0),
        place_map.transpose(0, 2, 1, 3),
    )
    return pl.pallas_call(
        functools.partial(kernel, subs, layers),
        out_shape=pltpu.VMEM((1, share, columns), jnp.float32),
        in_specs=[pl.BlockSpec(memory_space=pl.ANY)] * 5,
        out_specs=pl.BlockSpec(memory_space=pltpu.VMEM),
        scratch_shapes=[
            *[pltpu.SMEM(table.shape, table.dtype) for table in tables],
            pltpu.VMEM((tiles, bands, rows, rows), low),
            pltpu.VMEM((1, vectors, width + 2 * halo), low),
            pltpu.VMEM((tiles, vectors, rows), low),
            pltpu.VMEM((tiles + 2 * (bands // 2), columns, rows), low),
            pltpu.VMEM((tiles, vectors, rows), low),
            pltpu.VMEM((count, overlap, vectors, rows), low),
            pltpu.VMEM((count * (overlap + 1), vectors, rows), low),
            pltpu.VMEM((count * (overlap + 1), bands, vectors, rows), low),
            pltpu.VMEM((count, 2, vectors, halo), low),
            pltpu.VMEM((count, 2, vectors, halo), low),
            pltpu.SMEM((slots * tiles,), jnp.int32),
            pltpu.SMEM((count * 2 * (bands // 2),), jnp.int32),
            pltpu.SMEM((count * overlap,), jnp.int32),
            pltpu.VMEM((columns, columns), jnp.float32),
            pltpu.VMEM((columns, columns), low),
            pltpu.VMEM((layers - 1, share, columns), low),
            dma((4,)),
            dma((tiles,)),
            dma((count,)), dma((count,)),
            dma((2,)), dma((2,)),
            dma((count, 2)), dma((count, 2)),
            dma((layers - 1,)), dma((layers - 1,)),
        ],
        compiler_params=pltpu.CompilerParams(collective_id=0, has_side_effects=True),
    )(*tables, deflation, stiffness)


def solution(mesh):
    in_specs = (
        P("sub", "grp", None, None, None),
        P("sub", None, "grp"),
        P(),
        P(None, "grp", None, None),
        P("sub", "grp", None, None),
    )
    out_specs = P("sub", "grp", None)
    return jax.shard_map(
        functools.partial(on_device, mesh.shape["sub"], mesh.shape["grp"]),
        mesh=mesh,
        in_specs=in_specs,
        out_specs=out_specs,
        check_vma=False,
    )
```
